32 devices in a mesh: ctx: 8 (over z, x), shard: 4 (over y, core).
Axes of the slice: x: 2, y: 2, z: 4, core: 2. Of those that a mesh axis runs over, the one named last changes fastest.
Arguments:
- token_ids: int32 [4, 2048], P('shard', 'ctx'), may hold values from 0 to 31999
- targets: int32 [4, 2048], P('shard', 'ctx'), may hold values from 0 to 31999
- positions: int32 [4, 2048], P('shard', 'ctx'), may hold values from 0 to 1023, as said below
- embed_table: float32 [32000, 576], P(('ctx', 'shard')), may hold values from -0.52 to 0.52
- projection_weight: float32 [2, 576, 960], P(None, 'shard'), may hold values from -0.25 to 0.25
- w_out: float32 [2, 576, 576], P(None, 'shard'), may hold values from -1 to 1
- w_gate_up: float32 [2, 576, 3072], P(None, 'shard'), may hold values from -0.25 to 0.25
- w_down: float32 [2, 1536, 576], P(None, 'shard'), may hold values from -0.15625 to 0.15625
- norm_gains: float32 [5, 576], P(None, 'shard'), may hold values from 0.5 to 1.5
- table_mom: float32 [32000, 576], P(('ctx', 'shard')), may hold values from -3.0517578e-05 to 3.0517578e-05
- projection_momentum: float32 [2, 576, 960], P(None, 'shard'), may hold values from -0.00018310547 to 0.00018310547
- out_mom: float32 [2, 576, 576], P(None, 'shard'), may hold values from -0.00018310547 to 0.00018310547
- gate_up_mom: float32 [2, 576, 3072], P(None, 'shard'), may hold values from -0.00018310547 to 0.00018310547
- down_mom: float32 [2, 1536, 576], P(None, 'shard'), may hold values from -0.00018310547 to 0.00018310547
- gain_mom: float32 [5, 576], P(None, 'shard'), may hold values from -0.0029296875 to 0.0029296875
- table_avg: float32 [32000, 576], P(('ctx', 'shard')), may hold values from -0.48 to 0.48
- projection_average: float32 [2, 576, 960], P(None, 'shard'), may hold values from -0.25 to 0.25
- out_avg: float32 [2, 576, 576], P(None, 'shard'), may hold values from -1 to 1
- gate_up_avg: float32 [2, 576, 3072], P(None, 'shard'), may hold values from -0.25 to 0.25
- down_avg: float32 [2, 1536, 576], P(None, 'shard'), may hold values from -0.15625 to 0.15625
- gain_avg: float32 [5, 576], P(None, 'shard'), may hold values from 0.5 to 1.5
Outputs:
- mean_loss: float32 [], replicated
- grad_norm: float32 [], replicated
- new_table: float32 [32000, 576], P(('ctx', 'shard'))
- new_qkv: float32 [2, 576, 960], P(None, 'shard')
- new_out: float32 [2, 576, 576], P(None, 'shard')
- new_gate_up: float32 [2, 576, 3072], P(None, 'shard')
- new_down: float32 [2, 1536, 576], P(None, 'shard')
- new_gains: float32 [5, 576], P(None, 'shard')
- table_mom_new: float32 [32000, 576], P(('ctx', 'shard'))
- qkv_mom_new: float32 [2, 576, 960], P(None, 'shard')
- out_mom_new: float32 [2, 576, 576], P(None, 'shard')
- gate_up_mom_new: float32 [2, 576, 3072], P(None, 'shard')
- down_mom_new: float32 [2, 1536, 576], P(None, 'shard')
- gain_mom_new: float32 [5, 576], P(None, 'shard')
- table_avg_new: float32 [32000, 576], P(('ctx', 'shard'))
- qkv_avg_new: float32 [2, 576, 960], P(None, 'shard')
- out_avg_new: float32 [2, 576, 576], P(None, 'shard')
- gate_up_avg_new: float32 [2, 576, 3072], P(None, 'shard')
- down_avg_new: float32 [2, 1536, 576], P(None, 'shard')
- gain_avg_new: float32 [5, 576], P(None, 'shard')
The draws below stay inside these ranges and needn't reach their ends.
Inputs may be any that keep to these rules, and one draw needn't show every extreme that they name: `positions`: each sequence is a run of whole documents; a token's value counts the tokens before it in its own document, so every document begins with 0. No document is longer than 1024 tokens, and every sequence holds one of exactly 1024 tokens.
All inputs are finite; a program needn't handle non-finite values.
Results may differ from the reference program's by a relative error of at most 0.003.
The reference program's roundings to bfloat16 on the way count: a program that leaves them out, or rounds other values in their place, can miss the bound.
Values may be sent and summed in bfloat16 or wider, within the bound.
No kernel may reach another device: no remote copies, remote signals or barrier semaphores. Data moves between devices by JAX's collectives and lax.ppermute only.
A program may use at most 256 MiB of HBM per device.

```python
import math
import jax
import jax.numpy as jnp
import numpy as np
from jax import lax

MODEL_WIDTH = 576
QUERY_HEADS = 9
KEY_VALUE_HEADS = 3
HEAD_SIZE = 64
FF = 1536
V = 32000
LAYER_COUNT = 2
KEYS_PER_BLOCK = 512
SEQUENCE_LENGTH = 2048
DOC_CAP = 1024
N_SHARD = 4


def draw_positions(key, part):
    key_offset, key_cuts = jax.random.split(jax.random.fold_in(key, 7))
    indices = jnp.arange(SEQUENCE_LENGTH, dtype=jnp.int32)
    offset = jax.random.randint(key_offset, (N_SHARD, 1), 0, SEQUENCE_LENGTH - DOC_CAP + 1)
    cut_flags = jax.random.randint(key_cuts, (N_SHARD, SEQUENCE_LENGTH), 0, max(DOC_CAP // 4, 1)) == 0
    relative = indices[None, :] - offset
    inside = (relative > 0) & (relative < DOC_CAP)
    forced = relative % DOC_CAP == 0
    starts = cut_flags & jnp.logical_not(inside) | forced | (indices[None, :] == 0)
    last_start = lax.cummax(jnp.where(starts, indices[None, :], 0), axis=1)
    return (indices[None, :] - last_start).astype(jnp.int32)


def draw_embed_table(key, part):
    key_noise, key_sign = jax.random.split(jax.random.fold_in(key, 11))
    signs = jax.random.randint(key_sign, (1, MODEL_WIDTH), 0, 2).astype(jnp.float32) * 2.0 - 1.0
    noise = jnp.clip(0.08 * jax.random.normal(key_noise, (V, MODEL_WIDTH), jnp.float32), -0.48, 0.48)
    return (noise + 0.04 * signs).astype(jnp.float32)


def set_ends(array, own_key, smallest, top_value):
    spot = [jax.random.randint(jax.random.fold_in(own_key, axis), (), 0, length) for axis, length in enumerate(array.shape)]
    widest = array.shape.index(max(array.shape))
    neighbour = spot[:widest] + [(spot[widest] + 1) % array.shape[widest]] + spot[widest + 1:]
    return array.at[tuple(spot)].set(smallest).at[tuple(neighbour)].set(top_value)


def level_of(stream_key, extent, cuts, smallest, top_value):
    loudness = 1.0
    for position, parts in cuts:
        heights = jax.random.uniform(jax.random.fold_in(jax.random.fold_in(stream_key, 6), position), (parts,), jnp.float32, smallest / len(cuts), top_value / len(cuts))
        loudness = loudness * jnp.repeat(jnp.exp(heights), extent[position] // parts).reshape((-1,) + (1,) * (len(extent) - 1 - position))
    return loudness


def rank_table(count, lean):
    weights = [(1 << 20) // math.isqrt(grade ** lean) + 1 for grade in range(1, count + 1)]
    deviation = 1 + sum(weights) // (1 << 30)
    return np.cumsum(np.array([max(1, weight // deviation) for weight in weights]))


def ranked_ids(own_key, dims, amount, lean):
    listing = rank_table(amount, lean)
    ticket = jax.random.randint(jax.random.fold_in(own_key, 1), dims, 0, int(listing[amount - 1]))
    standing = jnp.searchsorted(jnp.asarray(listing, jnp.int32), ticket, side="right")
    return jax.random.permutation(jax.random.fold_in(own_key, 2), amount)[standing].astype(jnp.int32)


def scatter_about(rng, dims, deviation, limit, cuts=(), kind=jnp.bfloat16):
    gain = level_of(rng, dims, cuts, -0.22, 0.18) if cuts else 1.0
    result = jax.random.normal(rng, dims, jnp.float32) * deviation * gain
    return jnp.minimum(jnp.maximum(result, -limit), limit).astype(kind)


def setup_inputs(seed: int = 0) -> dict:
    key_of = jax.random.split(jax.random.key(seed), 22)
    return {
        "token_ids": set_ends(ranked_ids(key_of[0], (N_SHARD, SEQUENCE_LENGTH), V, 2), jax.random.fold_in(key_of[0], 3), 0, V - 1).astype(jnp.int32),
        "targets": set_ends(ranked_ids(key_of[1], (N_SHARD, SEQUENCE_LENGTH), V, 2), jax.random.fold_in(key_of[1], 3), 0, V - 1).astype(jnp.int32),
        "positions": draw_positions(jax.random.fold_in(key_of[21], 71), 0),
        "embed_table": draw_embed_table(jax.random.fold_in(key_of[21], 71), 0),
        "projection_weight": scatter_about(key_of[4], (LAYER_COUNT, MODEL_WIDTH, (QUERY_HEADS + 2 * KEY_VALUE_HEADS) * HEAD_SIZE), MODEL_WIDTH ** -0.5, 0.25, ((1, 4),), jnp.float32),
        "w_out": scatter_about(key_of[5], (LAYER_COUNT, QUERY_HEADS * HEAD_SIZE, MODEL_WIDTH), (QUERY_HEADS * HEAD_SIZE // 16) ** -0.5, 1.0, ((1, 4),), jnp.float32),
        "w_gate_up": scatter_about(key_of[6], (LAYER_COUNT, MODEL_WIDTH, 2 * FF), MODEL_WIDTH ** -0.5, 0.25, ((1, 4),), jnp.float32),
        "w_down": scatter_about(key_of[7], (LAYER_COUNT, FF, MODEL_WIDTH), FF ** -0.5, 0.15625, ((1, 4),), jnp.float32),
        "norm_gains": jnp.clip(1.0 + 0.1 * jax.random.normal(key_of[8], (2 * LAYER_COUNT + 1, MODEL_WIDTH), jnp.float32), 0.5, 1.5),
        "table_mom": scatter_about(key_of[9], (V, MODEL_WIDTH), 0.000005, 3.0517578125e-05, ((0, 32),), jnp.float32),
        "projection_momentum": scatter_about(key_of[10], (LAYER_COUNT, MODEL_WIDTH, (QUERY_HEADS + 2 * KEY_VALUE_HEADS) * HEAD_SIZE), 0.00003, 0.00018310547, ((1, 4),), jnp.float32),
        "out_mom": scatter_about(key_of[11], (LAYER_COUNT, QUERY_HEADS * HEAD_SIZE, MODEL_WIDTH), 0.00003, 0.00018310547, ((1, 4),), jnp.float32),
        "gate_up_mom": scatter_about(key_of[12], (LAYER_COUNT, MODEL_WIDTH, 2 * FF), 0.00003, 0.00018310547, ((1, 4),), jnp.float32),
        "down_mom": scatter_about(key_of[13], (LAYER_COUNT, FF, MODEL_WIDTH), 0.00003, 0.00018310547, ((1, 4),), jnp.float32),
        "gain_mom": scatter_about(key_of[14], (2 * LAYER_COUNT + 1, MODEL_WIDTH), 0.0005, 0.0029296875, ((1, 4),), jnp.float32),
        "table_avg": scatter_about(key_of[15], (V, MODEL_WIDTH), 0.08, 0.48, ((0, 32),), jnp.float32),
        "projection_average": scatter_about(key_of[16], (LAYER_COUNT, MODEL_WIDTH, (QUERY_HEADS + 2 * KEY_VALUE_HEADS) * HEAD_SIZE), MODEL_WIDTH ** -0.5, 0.25, ((1, 4),), jnp.float32),
        "out_avg": scatter_about(key_of[17], (LAYER_COUNT, QUERY_HEADS * HEAD_SIZE, MODEL_WIDTH), (QUERY_HEADS * HEAD_SIZE // 16) ** -0.5, 1.0, ((1, 4),), jnp.float32),
        "gate_up_avg": scatter_about(key_of[18], (LAYER_COUNT, MODEL_WIDTH, 2 * FF), MODEL_WIDTH ** -0.5, 0.25, ((1, 4),), jnp.float32),
        "down_avg": scatter_about(key_of[19], (LAYER_COUNT, FF, MODEL_WIDTH), FF ** -0.5, 0.15625, ((1, 4),), jnp.float32),
        "gain_avg": jnp.clip(1.0 + 0.1 * jax.random.normal(key_of[20], (2 * LAYER_COUNT + 1, MODEL_WIDTH), jnp.float32), 0.5, 1.5),
    }


SMOOTH = 0.1
Z_WEIGHT = 0.0001
CLIP_NORM = 0.08
LEARN_RATE = 100.0
MOMENTUM = 0.5
AVG_DECAY = 0.5
SCORE_SCALE = 0.125
HIDDEN_SCORE = -1e+30
EPSILON = 1e-05
PRECISE = lax.Precision.HIGHEST

@jax.custom_vjp
def lower_precision(v):
    return lax.optimization_barrier(v.astype(jnp.bfloat16)).astype(jnp.float32)

@jax.custom_vjp
def low_back(v):
    return v

def low_keep(v):
    return (lower_precision(v), None)

def low_pass(kept, grad):
    return (grad,)

def back_keep(v):
    return (v, None)

def back_low(kept, grad):
    return (lower_precision(grad),)
lower_precision.defvjp(low_keep, low_pass)
low_back.defvjp(back_keep, back_low)

def normed(values, gain_row):
    return values * lax.rsqrt(lax.optimization_barrier(jnp.mean(values * values, axis=-1, keepdims=True)) + EPSILON) * gain_row

def rotary(position_row):
    half_dim = HEAD_SIZE // 2
    inv_freq = 10000.0 ** (-jnp.arange(half_dim, dtype=jnp.float32) / half_dim)
    angles = position_row.astype(jnp.float32)[:, None, None] * inv_freq
    return (jnp.cos(angles), jnp.sin(angles))

def rotary_apply(values, cosine_table, sine_values):
    half_dim = HEAD_SIZE // 2
    first_half = values[..., :half_dim]
    second = values[..., half_dim:]
    return jnp.concatenate([first_half * cosine_table - second * sine_values, second * cosine_table + first_half * sine_values], axis=-1)

def swiglu(gate_up):
    return jax.nn.silu(gate_up[:, :FF]) * gate_up[:, FF:]

def attention_layer(query_batch, key_b, value_b, query_position, document_begin):
    block_list = SEQUENCE_LENGTH // KEYS_PER_BLOCK
    key_index = jnp.arange(SEQUENCE_LENGTH)

    def single_block(block_item):
        query_blk, index_blk, start_blk = block_item
        scores = jnp.einsum('qgrd,kgd->grqk', query_blk, key_b, precision=PRECISE) * SCORE_SCALE
        scores = low_back(scores)
        visible = (key_index[None, :] <= index_blk[:, None]) & (key_index[None, :] >= start_blk[:, None])
        attn_prob = lower_precision(jax.nn.softmax(jnp.where(visible, scores, HIDDEN_SCORE), axis=-1))
        return jnp.einsum('grqk,kgd->qgrd', attn_prob, value_b, precision=PRECISE)
    layer_output = lax.map(jax.checkpoint(single_block), (query_batch.reshape(block_list, KEYS_PER_BLOCK, KEY_VALUE_HEADS, QUERY_HEADS // KEY_VALUE_HEADS, HEAD_SIZE), query_position.reshape(block_list, KEYS_PER_BLOCK), document_begin.reshape(block_list, KEYS_PER_BLOCK)))
    return layer_output.reshape(SEQUENCE_LENGTH, QUERY_HEADS * HEAD_SIZE)

def token_losses(final_b, table_b, target_row):
    block_list = SEQUENCE_LENGTH // KEYS_PER_BLOCK

    def single_block(block_item):
        hidden_blk, target_blk = block_item
        logits = low_back(jnp.dot(hidden_blk, table_b.T, precision=PRECISE))
        log_total = jax.nn.logsumexp(logits, axis=-1)
        picked = jnp.take_along_axis(logits, target_blk[:, None], axis=1)[:, 0]
        per_token = log_total - (1.0 - SMOOTH) * picked - SMOOTH * lax.optimization_barrier(jnp.mean(logits, axis=-1)) + Z_WEIGHT * log_total * log_total
        return jnp.sum(per_token)
    return jnp.sum(lax.map(jax.checkpoint(single_block), (final_b.reshape(block_list, KEYS_PER_BLOCK, MODEL_WIDTH), target_row.reshape(block_list, KEYS_PER_BLOCK))))

def sequence_loss(weights_b, ids_row, target_row, position_row):
    table_b, qkv_b, out_b, gate_up_b, down_b, gains_b = weights_b
    cosine_table, sine_values = rotary(position_row)
    query_position = jnp.arange(SEQUENCE_LENGTH)
    document_begin = query_position - position_row
    head_groups = QUERY_HEADS // KEY_VALUE_HEADS
    hidden = table_b[ids_row]
    for layer_id in range(LAYER_COUNT):
        attn_in = lower_precision(normed(hidden, gains_b[2 * layer_id]))
        projected_rows = low_back(jnp.dot(attn_in, qkv_b[layer_id], precision=PRECISE))
        query_rows = rotary_apply(projected_rows[:, :QUERY_HEADS * HEAD_SIZE].reshape(SEQUENCE_LENGTH, QUERY_HEADS, HEAD_SIZE), cosine_table, sine_values)
        key_portion = rotary_apply(projected_rows[:, QUERY_HEADS * HEAD_SIZE:(QUERY_HEADS + KEY_VALUE_HEADS) * HEAD_SIZE].reshape(SEQUENCE_LENGTH, KEY_VALUE_HEADS, HEAD_SIZE), cosine_table, sine_values)
        value_portion = projected_rows[:, (QUERY_HEADS + KEY_VALUE_HEADS) * HEAD_SIZE:].reshape(SEQUENCE_LENGTH, KEY_VALUE_HEADS, HEAD_SIZE)
        attended_output = attention_layer(lower_precision(query_rows).reshape(SEQUENCE_LENGTH, KEY_VALUE_HEADS, head_groups, HEAD_SIZE), lower_precision(key_portion), lower_precision(value_portion), query_position, document_begin)
        attended_output = lower_precision(low_back(attended_output))
        hidden = hidden + low_back(jnp.dot(attended_output, out_b[layer_id], precision=PRECISE))
        mlp_in = lower_precision(normed(hidden, gains_b[2 * layer_id + 1]))
        gate_up = low_back(jnp.dot(mlp_in, gate_up_b[layer_id], precision=PRECISE))
        hidden = hidden + low_back(jnp.dot(lower_precision(swiglu(gate_up)), down_b[layer_id], precision=PRECISE))
    final_b = lower_precision(normed(hidden, gains_b[2 * LAYER_COUNT]))
    return token_losses(final_b, table_b, target_row)

def advance(weight, grad_one, moment, average, factor):
    clipped = grad_one * factor
    moment_new = MOMENTUM * moment + clipped
    weight_new = weight - LEARN_RATE * (clipped + MOMENTUM * moment_new)
    return (weight_new, moment_new, AVG_DECAY * average + (1.0 - AVG_DECAY) * weight_new)

def reference(token_ids, targets, positions, embed_table, projection_weight, w_out, w_gate_up, w_down, norm_gains, table_mom, projection_momentum, out_mom, gate_up_mom, down_mom, gain_mom, table_avg, projection_average, out_avg, gate_up_avg, down_avg, gain_avg):
    params = (embed_table, projection_weight, w_out, w_gate_up, w_down, norm_gains)

    def total_loss(param_set):
        weights_b = tuple((lower_precision(param_one) for param_one in param_set))

        def one_sequence(carry, seq_item):
            ids_row, target_row, position_row = seq_item
            return (carry + sequence_loss(weights_b, ids_row, target_row, position_row), None)
        summed, _ = lax.scan(one_sequence, jnp.zeros((), jnp.float32), (token_ids, targets, positions))
        return summed / (N_SHARD * SEQUENCE_LENGTH)
    loss_value, pullback = jax.vjp(total_loss, params)
    gradients = pullback(jnp.ones((), jnp.float32))[0]
    square_sum = sum((jnp.sum(grad_one * grad_one) for grad_one in gradients))
    grad_norm = jnp.sqrt(square_sum)
    factor = CLIP_NORM / jnp.maximum(grad_norm, CLIP_NORM)
    moments = (table_mom, projection_momentum, out_mom, gate_up_mom, down_mom, gain_mom)
    averages = (table_avg, projection_average, out_avg, gate_up_avg, down_avg, gain_avg)
    results = [advance(params[number], gradients[number], moments[number], averages[number], factor) for number in range(6)]
    return (loss_value, grad_norm, results[0][0], results[1][0], results[2][0], results[3][0], results[4][0], results[5][0], results[0][1], results[1][1], results[2][1], results[3][1], results[4][1], results[5][1], results[0][2], results[1][2], results[2][2], results[3][2], results[4][2], results[5][2])
```

```python
import jax
import jax.numpy as jnp
from jax import lax
from jax.experimental import pallas as pl
from jax.experimental.pallas import tpu as pltpu
from jax.sharding import PartitionSpec as P

MODEL_WIDTH = 576
QUERY_HEADS = 9
KEY_VALUE_HEADS = 3
HEAD_SIZE = 64
FF = 1536
V = 32000
LAYER_COUNT = 2
GROUPS = QUERY_HEADS // KEY_VALUE_HEADS


SMOOTH = 0.1
Z_WEIGHT = 0.0001
CLIP_NORM = 0.08
LEARN_RATE = 100.0
MOMENTUM = 0.5
AVG_DECAY = 0.5
SCORE_SCALE = 0.125
HIDDEN_SCORE = -1e30
EPSILON = 1e-05
HALF_TYPE = jnp.bfloat16
WIDE_NUMBER_TYPE = jnp.float32


def normed(values, gain_row):
    return (
        values * lax.rsqrt(jnp.mean(values * values, axis=-1, keepdims=True) + EPSILON) * gain_row
    )


def rotary(position_row):
    half_dim = HEAD_SIZE // 2
    inv_freq = 10000.0 ** (-jnp.arange(half_dim, dtype=jnp.float32) / half_dim)
    angles = position_row.astype(jnp.float32)[:, None, None] * inv_freq
    return (jnp.cos(angles), jnp.sin(angles))


def rotary_apply(values, cosine_table, sine_values):
    half_dim = HEAD_SIZE // 2
    first_half = values[..., :half_dim]
    second = values[..., half_dim:]
    return jnp.concatenate(
        [
            first_half * cosine_table - second * sine_values,
            second * cosine_table + first_half * sine_values,
        ],
        axis=-1,
    )


def rotate_back(grads_in, cosine_table, sine_values):
    half_dim = HEAD_SIZE // 2
    first_half = grads_in[..., :half_dim]
    second = grads_in[..., half_dim:]
    return jnp.concatenate(
        [
            first_half * cosine_table + second * sine_values,
            second * cosine_table - first_half * sine_values,
        ],
        axis=-1,
    )


def swiglu(gate_up):
    return jax.nn.silu(gate_up[:, :FF]) * gate_up[:, FF:]


def contract(left_side, right_side, left_dim, right_dim):
    return lax.dot_general(
        left_side,
        right_side,
        (((left_dim,), (right_dim,)), ((), ())),
        preferred_element_type=WIDE_NUMBER_TYPE,
    )


def butterfly(values, axis, combine):
    count = lax.axis_size(axis)
    step = 1
    while step < count:
        other = lax.ppermute(values, axis, [(i, i ^ step) for i in range(count)])
        values = combine(values, other)
        step *= 2
    return values


def add_all(values, axes):
    for axis in axes:
        values = butterfly(values, axis, jnp.add)
    return values


def exchange_sum(partial, axis):
    count = lax.axis_size(axis)
    index = lax.axis_index(axis)
    rows = partial.shape[0] // count

    def block(which):
        return lax.dynamic_slice_in_dim(partial, which * rows, rows, axis=0)

    total = block(index)
    for step in range(1, count):
        sent = lax.ppermute(
            block(index ^ step).astype(HALF_TYPE), axis, [(i, i ^ step) for i in range(count)]
        )
        total = total + sent.astype(WIDE_NUMBER_TYPE)
    return total


def window_visible(position_column, key_rows):
    rows = position_column.shape[0]
    base = key_rows - rows
    query_at = lax.broadcasted_iota(jnp.int32, (rows, key_rows), 0) + base
    key_at = lax.broadcasted_iota(jnp.int32, (rows, key_rows), 1)
    return (key_at <= query_at) & (key_at >= query_at - position_column)


def head_slice(head):
    return slice(head * HEAD_SIZE, (head + 1) * HEAD_SIZE)


def attend_kernel(query_ref, key_ref, value_ref, position_ref, out_ref, total_ref):
    key_rows = key_ref.shape[0]
    visible = window_visible(position_ref[...], key_rows)
    for head in range(QUERY_HEADS):
        group = head // GROUPS
        scores = (
            contract(query_ref[:, head_slice(head)], key_ref[:, head_slice(group)], 1, 1)
            * SCORE_SCALE
        )
        scores = jnp.where(visible, scores, HIDDEN_SCORE)
        row_max = jnp.max(scores, axis=1, keepdims=True)
        terms = jnp.exp(scores - row_max)
        row_sum = jnp.sum(terms, axis=1, keepdims=True)
        prob = (terms * (1.0 / row_sum)).astype(HALF_TYPE)
        out_ref[:, head_slice(head)] = contract(
            prob, value_ref[:, head_slice(group)], 1, 0
        ).astype(HALF_TYPE)
        total_ref[:, head : head + 1] = row_max + jnp.log(row_sum)


def attend(query, keys, values, position_column):
    rows = query.shape[0]
    return pl.pallas_call(
        attend_kernel,
        out_shape=(
            jax.ShapeDtypeStruct((rows, QUERY_HEADS * HEAD_SIZE), HALF_TYPE),
            jax.ShapeDtypeStruct((rows, 16), WIDE_NUMBER_TYPE),
        ),
        compiler_params=pltpu.CompilerParams(vmem_limit_bytes=48 << 20),
        name="attend",
    )(query, keys, values, position_column)


def attend_back_kernel(
    query_ref, key_ref, value_ref, total_ref, grad_ref, position_ref, dq_ref, dkv_ref
):
    key_rows = key_ref.shape[0]
    width = KEY_VALUE_HEADS * HEAD_SIZE
    visible = window_visible(position_ref[...], key_rows)
    for group in range(KEY_VALUE_HEADS):
        keys = key_ref[:, head_slice(group)]
        values = value_ref[:, head_slice(group)]
        key_grad = None
        value_grad = None
        for head in range(group * GROUPS, (group + 1) * GROUPS):
            query = query_ref[:, head_slice(head)]
            grad = grad_ref[:, head_slice(head)]
            scores = contract(query, keys, 1, 1) * SCORE_SCALE
            prob = jnp.where(visible, jnp.exp(scores - total_ref[:, head : head + 1]), 0.0)
            grad_prob = contract(grad, values, 1, 1)
            delta = jnp.sum(prob * grad_prob, axis=1, keepdims=True)
            grad_score = (prob * (grad_prob - delta)).astype(HALF_TYPE)
            dq_ref[:, head_slice(head)] = contract(grad_score, keys, 1, 0) * SCORE_SCALE
            key_part = contract(grad_score, query, 0, 0)
            value_part = contract(prob.astype(HALF_TYPE), grad, 0, 0)
            key_grad = key_part if key_grad is None else key_grad + key_part
            value_grad = value_part if value_grad is None else value_grad + value_part
        dkv_ref[:, head_slice(group)] = key_grad * SCORE_SCALE
        dkv_ref[:, width + group * HEAD_SIZE : width + (group + 1) * HEAD_SIZE] = value_grad


def attend_back(query, keys, values, totals, grads, position_column):
    rows = query.shape[0]
    return pl.pallas_call(
        attend_back_kernel,
        out_shape=(
            jax.ShapeDtypeStruct((rows, QUERY_HEADS * HEAD_SIZE), WIDE_NUMBER_TYPE),
            jax.ShapeDtypeStruct(
                (keys.shape[0], 2 * KEY_VALUE_HEADS * HEAD_SIZE), WIDE_NUMBER_TYPE
            ),
        ),
        compiler_params=pltpu.CompilerParams(vmem_limit_bytes=48 << 20),
        name="attend_back",
    )(query, keys, values, totals, grads, position_column)


def stats_kernel(final_ref, target_ref, table_ref, out_ref):
    logits = contract(final_ref[...], table_ref[...], 1, 1)
    row_max = jnp.max(logits, axis=1, keepdims=True)
    exp_sum = jnp.sum(jnp.exp(logits - row_max), axis=1, keepdims=True)
    logit_sum = jnp.sum(logits, axis=1, keepdims=True)
    column = lax.broadcasted_iota(jnp.int32, logits.shape, 1)
    chosen = jnp.sum(jnp.where(column == target_ref[...], logits, 0.0), axis=1, keepdims=True)
    out_ref[:, 0:1] = row_max
    out_ref[:, 1:2] = exp_sum
    out_ref[:, 2:3] = logit_sum
    out_ref[:, 3:4] = chosen


TOKEN_TILE = 256


def vocab_stats(finals, target_column, table_rows):
    tokens = finals.shape[0]
    tile = TOKEN_TILE
    return pl.pallas_call(
        stats_kernel,
        grid=(tokens // tile,),
        in_specs=[
            pl.BlockSpec((tile, MODEL_WIDTH), lambda i: (i, 0)),
            pl.BlockSpec((tile, 1), lambda i: (i, 0)),
            pl.BlockSpec(table_rows.shape, lambda i: (0, 0), pipeline_mode=pl.Buffered(1)),
        ],
        out_specs=pl.BlockSpec((tile, 4), lambda i: (i, 0)),
        out_shape=jax.ShapeDtypeStruct((tokens, 4), WIDE_NUMBER_TYPE),
        compiler_params=pltpu.CompilerParams(vmem_limit_bytes=56 << 20),
        name="vocab_stats",
    )(finals, target_column, table_rows)


def vocab_grad_kernel(all_tokens, final_ref, target_ref, lse_ref, table_ref, dx_ref, dw_ref):
    finals = final_ref[...]
    table = table_ref[...]
    logits = contract(finals, table, 1, 1)
    lse = lse_ref[...]
    column = lax.broadcasted_iota(jnp.int32, logits.shape, 1)
    grad = (
        jnp.exp(logits - lse) * (1.0 + 2.0 * Z_WEIGHT * lse)
        - jnp.where(column == target_ref[...], 1.0 - SMOOTH, 0.0)
        - SMOOTH / V
    ) / all_tokens
    grad = grad.astype(HALF_TYPE)
    dx_ref[...] = contract(grad, table, 1, 0)
    part = contract(grad, finals, 0, 0)

    @pl.when(pl.program_id(0) == 0)
    def _():
        dw_ref[...] = part

    @pl.when(pl.program_id(0) > 0)
    def _():
        dw_ref[...] += part


def vocab_grad(finals, target_column, lse_column, table_rows, all_tokens):
    tokens = finals.shape[0]
    tile = TOKEN_TILE

    def body(*refs):
        vocab_grad_kernel(all_tokens, *refs)

    return pl.pallas_call(
        body,
        grid=(tokens // tile,),
        in_specs=[
            pl.BlockSpec((tile, MODEL_WIDTH), lambda i: (i, 0)),
            pl.BlockSpec((tile, 1), lambda i: (i, 0)),
            pl.BlockSpec((tile, 1), lambda i: (i, 0)),
            pl.BlockSpec(table_rows.shape, lambda i: (0, 0), pipeline_mode=pl.Buffered(1)),
        ],
        out_specs=(
            pl.BlockSpec((tile, MODEL_WIDTH), lambda i: (i, 0)),
            pl.BlockSpec(table_rows.shape, lambda i: (0, 0), pipeline_mode=pl.Buffered(1)),
        ),
        out_shape=(
            jax.ShapeDtypeStruct((tokens, MODEL_WIDTH), WIDE_NUMBER_TYPE),
            jax.ShapeDtypeStruct(table_rows.shape, WIDE_NUMBER_TYPE),
        ),
        compiler_params=pltpu.CompilerParams(vmem_limit_bytes=60 << 20),
        name="vocab_grad",
    )(finals, target_column, lse_column, table_rows)


def advance(weight, grad_one, moment, average, factor):
    clipped = grad_one * factor
    moment_new = MOMENTUM * moment + clipped
    weight_new = weight - LEARN_RATE * (clipped + MOMENTUM * moment_new)
    return (weight_new, moment_new, AVG_DECAY * average + (1.0 - AVG_DECAY) * weight_new)


def shards(
    token_ids,
    targets,
    positions,
    embed_table,
    projection_weight,
    w_out,
    w_gate_up,
    w_down,
    norm_gains,
    table_mom,
    projection_momentum,
    out_mom,
    gate_up_mom,
    down_mom,
    gain_mom,
    table_avg,
    projection_average,
    out_avg,
    gate_up_avg,
    down_avg,
    gain_avg,
):
    ctx_count = lax.axis_size("ctx")
    shard_count = lax.axis_size("shard")
    ctx_index = lax.axis_index("ctx")
    shard_index = lax.axis_index("shard")
    token_rows = token_ids.shape[1]
    own_rows = embed_table.shape[0]
    sequence = token_rows * ctx_count
    all_tokens = sequence * shard_count
    query_span_width = QUERY_HEADS * HEAD_SIZE
    key_value_width = KEY_VALUE_HEADS * HEAD_SIZE
    back = ctx_count // 2

    table_rows = lax.all_gather(embed_table.astype(HALF_TYPE), "shard", axis=0, tiled=True)
    slice_rows = table_rows.shape[0]
    pairs = lax.all_gather(
        jnp.concatenate([token_ids, targets], axis=0), ("ctx", "shard"), axis=0
    ).reshape(ctx_count, shard_count, 2, token_rows)
    every_id = pairs[:, :, 0].reshape(all_tokens)
    sequence_pairs = lax.dynamic_index_in_dim(pairs, shard_index, axis=1, keepdims=False)
    first_row = ctx_index * slice_rows
    id_row = sequence_pairs[:, 0].reshape(sequence) - first_row
    target_column = sequence_pairs[:, 1].reshape(sequence, 1) - first_row
    id_here = (id_row >= 0) & (id_row < slice_rows)
    picked = jnp.where(
        id_here[:, None], table_rows[jnp.where(id_here, id_row, 0)], jnp.zeros((), HALF_TYPE)
    )
    looked_up = lax.all_to_all(
        picked.reshape(ctx_count, token_rows, MODEL_WIDTH), "ctx", 0, 0, tiled=True
    )
    hidden = jnp.sum(looked_up.astype(WIDE_NUMBER_TYPE), axis=0)
    position_row = positions[0]
    position_column = position_row[:, None]
    cosine_table, sine_values = rotary(position_row)
    gain_values = lax.all_gather(
        norm_gains.astype(HALF_TYPE), "shard", axis=1, tiled=True
    ).astype(WIDE_NUMBER_TYPE)

    def gathered(weight, layer_id):
        return lax.all_gather(weight[layer_id].astype(HALF_TYPE), "shard", axis=0, tiled=True)

    fetched = [
        tuple(gathered(weight, layer_id) for weight in (projection_weight, w_out, w_gate_up, w_down))
        for layer_id in range(LAYER_COUNT)
    ]

    saved_state = []
    for layer_id in range(LAYER_COUNT):
        qkv_full, out_full, gate_up_full, down_full = fetched[layer_id]
        layer_input = hidden
        attn_in = normed(hidden, gain_values[2 * layer_id]).astype(HALF_TYPE)
        projected_kv = jnp.dot(
            attn_in, qkv_full[:, query_span_width:], preferred_element_type=WIDE_NUMBER_TYPE
        )
        key_rows = (
            rotary_apply(
                projected_kv[:, :key_value_width].reshape(token_rows, KEY_VALUE_HEADS, HEAD_SIZE),
                cosine_table,
                sine_values,
            )
            .astype(HALF_TYPE)
            .reshape(token_rows, key_value_width)
        )
        own_kv = jnp.concatenate(
            [key_rows, projected_kv[:, key_value_width:].astype(HALF_TYPE)], axis=1
        )
        window = [
            lax.ppermute(own_kv, "ctx", [(i, i + step) for i in range(ctx_count - step)])
            for step in range(back, 0, -1)
        ]
        window_kv = jnp.concatenate(window + [own_kv], axis=0)
        window_keys = window_kv[:, :key_value_width]
        window_values = window_kv[:, key_value_width:]
        projected_query = jnp.dot(
            attn_in, qkv_full[:, :query_span_width], preferred_element_type=WIDE_NUMBER_TYPE
        )
        query = (
            rotary_apply(
                projected_query.reshape(token_rows, QUERY_HEADS, HEAD_SIZE),
                cosine_table,
                sine_values,
            )
            .astype(HALF_TYPE)
            .reshape(token_rows, query_span_width)
        )
        attn_out, log_total = attend(query, window_keys, window_values, position_column)
        hidden = hidden + jnp.dot(attn_out, out_full, preferred_element_type=WIDE_NUMBER_TYPE)
        middle = hidden
        mlp_in = normed(hidden, gain_values[2 * layer_id + 1]).astype(HALF_TYPE)
        gate_up = jnp.dot(mlp_in, gate_up_full, preferred_element_type=WIDE_NUMBER_TYPE)
        act_half = swiglu(gate_up).astype(HALF_TYPE)
        hidden = hidden + jnp.dot(act_half, down_full, preferred_element_type=WIDE_NUMBER_TYPE)
        saved_state.append(
            (
                layer_input,
                middle,
                query,
                window_keys,
                window_values,
                log_total,
                attn_out,
                attn_in,
                mlp_in,
                gate_up,
                act_half,
            )
        )
    final_gain = gain_values[2 * LAYER_COUNT]
    final_half = normed(hidden, final_gain).astype(HALF_TYPE)
    sequence_final = lax.all_gather(final_half, "ctx", axis=0, tiled=True)

    def combine(first_stats, second_stats):
        joint_max = jnp.maximum(first_stats[0], second_stats[0])
        return jnp.stack(
            [
                joint_max,
                first_stats[1] * jnp.exp(first_stats[0] - joint_max)
                + second_stats[1] * jnp.exp(second_stats[0] - joint_max),
                first_stats[2] + second_stats[2],
                first_stats[3] + second_stats[3],
            ]
        )

    stats = vocab_stats(sequence_final, target_column, table_rows).T
    stats = butterfly(stats, "ctx", combine)
    row_lse = stats[0] + jnp.log(stats[1])
    token_loss = (
        row_lse
        - (1.0 - SMOOTH) * stats[3]
        - SMOOTH * stats[2] / V
        + Z_WEIGHT * row_lse * row_lse
    )
    own_loss = (
        jnp.sum(lax.dynamic_slice_in_dim(token_loss, ctx_index * token_rows, token_rows))
        / all_tokens
    )
    hidden_grad_parts, slice_grad = vocab_grad(
        sequence_final, target_column, row_lse[:, None], table_rows, all_tokens
    )
    hidden_grad = lax.psum_scatter(hidden_grad_parts, "ctx", scatter_dimension=0, tiled=True)
    table_grad = exchange_sum(slice_grad, "shard")
    _, final_back = jax.vjp(normed, hidden, final_gain)
    grad_hidden, grad_final_gain = final_back(hidden_grad)
    layer_grads = [None] * LAYER_COUNT
    gain_rows = [None] * (2 * LAYER_COUNT) + [grad_final_gain]
    for layer_id in reversed(range(LAYER_COUNT)):
        (
            layer_input,
            middle,
            query,
            window_keys,
            window_values,
            log_total,
            attn_out,
            attn_in,
            mlp_in,
            gate_up,
            act_half,
        ) = saved_state[layer_id]
        qkv_full, out_full, gate_up_full, down_full = fetched[layer_id]
        _, mlp_back = jax.vjp(normed, middle, gain_values[2 * layer_id + 1])
        _, act_back = jax.vjp(swiglu, gate_up)
        out_grad = grad_hidden.astype(HALF_TYPE)
        grad_down = contract(act_half, out_grad, 0, 0)
        grad_act = contract(out_grad, down_full, 1, 1)
        grad_gate_up = act_back(grad_act)[0].astype(HALF_TYPE)
        grad_gu_weight = contract(mlp_in, grad_gate_up, 0, 0)
        grad_middle, gain_rows[2 * layer_id + 1] = mlp_back(
            contract(grad_gate_up, gate_up_full, 1, 1)
        )
        grad_hidden = grad_hidden + grad_middle
        branch_grad = grad_hidden.astype(HALF_TYPE)
        grad_out_weight = contract(attn_out, branch_grad, 0, 0)
        grad_attended = contract(branch_grad, out_full, 1, 1).astype(HALF_TYPE)
        query_gradient, window_grad = attend_back(
            query, window_keys, window_values, log_total, grad_attended, position_column
        )
        key_value_gradient = window_grad[back * token_rows :]
        for step in range(1, back + 1):
            part = window_grad[(back - step) * token_rows : (back - step + 1) * token_rows]
            key_value_gradient = key_value_gradient + lax.ppermute(
                part.astype(HALF_TYPE), "ctx", [(i + step, i) for i in range(ctx_count - step)]
            ).astype(WIDE_NUMBER_TYPE)
        _, attn_back = jax.vjp(normed, layer_input, gain_values[2 * layer_id])
        grad_projected = jnp.concatenate(
            [
                rotate_back(
                    query_gradient.reshape(token_rows, QUERY_HEADS, HEAD_SIZE),
                    cosine_table,
                    sine_values,
                ).reshape(token_rows, query_span_width),
                rotate_back(
                    key_value_gradient[:, :key_value_width].reshape(
                        token_rows, KEY_VALUE_HEADS, HEAD_SIZE
                    ),
                    cosine_table,
                    sine_values,
                ).reshape(token_rows, key_value_width),
                key_value_gradient[:, key_value_width:],
            ],
            axis=1,
        ).astype(HALF_TYPE)
        grad_qkv_weight = contract(attn_in, grad_projected, 0, 0)
        grad_input, gain_rows[2 * layer_id] = attn_back(contract(grad_projected, qkv_full, 1, 1))
        grad_hidden = grad_hidden + grad_input
        mlp_grads = lax.psum(
            (exchange_sum(grad_gu_weight, "shard"), exchange_sum(grad_down, "shard")), "ctx"
        )
        attn_grads = lax.psum(
            (exchange_sum(grad_qkv_weight, "shard"), exchange_sum(grad_out_weight, "shard")), "ctx"
        )
        layer_grads[layer_id] = attn_grads + mlp_grads
    every_grad = lax.all_gather(
        grad_hidden.astype(HALF_TYPE), ("ctx", "shard"), axis=0, tiled=True
    )
    own_first = (ctx_index * shard_count + shard_index) * own_rows
    chosen_rows = (own_first + jnp.arange(own_rows))[:, None] == every_id[None, :]
    table_grad = table_grad + contract(chosen_rows.astype(HALF_TYPE), every_grad, 1, 0)
    gain_total = add_all(jnp.stack(gain_rows), ("ctx", "shard"))
    gain_width = norm_gains.shape[1]
    gain_grad = lax.dynamic_slice_in_dim(gain_total, shard_index * gain_width, gain_width, axis=1)
    qkv_grad, out_grad_all, gate_up_grad, down_grad = [
        jnp.stack([layer_grads[layer_no][which] for layer_no in range(LAYER_COUNT)])
        for which in range(4)
    ]
    layer_square = sum(
        (
            jnp.sum(grad_one * grad_one)
            for grad_one in (qkv_grad, out_grad_all, gate_up_grad, down_grad, gain_grad)
        )
    )
    sums = add_all(
        jnp.stack([own_loss, layer_square / ctx_count + jnp.sum(table_grad * table_grad)]),
        ("ctx", "shard"),
    )
    loss_sum, square_sum = sums[0], sums[1]
    grad_norm = jnp.sqrt(square_sum)
    factor = CLIP_NORM / jnp.maximum(grad_norm, CLIP_NORM)
    table_new = advance(embed_table, table_grad, table_mom, table_avg, factor)
    qkv_new = advance(projection_weight, qkv_grad, projection_momentum, projection_average, factor)
    out_new = advance(w_out, out_grad_all, out_mom, out_avg, factor)
    gate_up_new = advance(w_gate_up, gate_up_grad, gate_up_mom, gate_up_avg, factor)
    down_new = advance(w_down, down_grad, down_mom, down_avg, factor)
    gains_new = advance(norm_gains, gain_grad, gain_mom, gain_avg, factor)
    return (
        loss_sum,
        grad_norm,
        table_new[0],
        qkv_new[0],
        out_new[0],
        gate_up_new[0],
        down_new[0],
        gains_new[0],
        table_new[1],
        qkv_new[1],
        out_new[1],
        gate_up_new[1],
        down_new[1],
        gains_new[1],
        table_new[2],
        qkv_new[2],
        out_new[2],
        gate_up_new[2],
        down_new[2],
        gains_new[2],
    )


def solution(mesh):
    return jax.shard_map(
        shards,
        mesh=mesh,
        in_specs=(
            P("shard", "ctx"),
            P("shard", "ctx"),
            P("shard", "ctx"),
            P(("ctx", "shard"), None),
            P(None, "shard", None),
            P(None, "shard", None),
            P(None, "shard", None),
            P(None, "shard", None),
            P(None, "shard"),
            P(("ctx", "shard"), None),
            P(None, "shard", None),
            P(None, "shard", None),
            P(None, "shard", None),
            P(None, "shard", None),
            P(None, "shard"),
            P(("ctx", "shard"), None),
            P(None, "shard", None),
            P(None, "shard", None),
            P(None, "shard", None),
            P(None, "shard", None),
            P(None, "shard"),
        ),
        out_specs=(
            P(),
            P(),
            P(("ctx", "shard"), None),
            P(None, "shard", None),
            P(None, "shard", None),
            P(None, "shard", None),
            P(None, "shard", None),
            P(None, "shard"),
            P(("ctx", "shard"), None),
            P(None, "shard", None),
            P(None, "shard", None),
            P(None, "shard", None),
            P(None, "shard", None),
            P(None, "shard"),
            P(("ctx", "shard"), None),
            P(None, "shard", None),
            P(None, "shard", None),
            P(None, "shard", None),
            P(None, "shard", None),
            P(None, "shard"),
        ),
        check_vma=False,
    )
```

```python
import jax
import jax.numpy as jnp
from jax import lax
from jax.experimental import pallas as pl
from jax.experimental.pallas import tpu as pltpu
from jax.sharding import PartitionSpec as P

MODEL_WIDTH = 576
QUERY_HEADS = 9
KEY_VALUE_HEADS = 3
HEAD_SIZE = 64
FF = 1536
V = 32000
LAYER_COUNT = 2
GROUPS = QUERY_HEADS // KEY_VALUE_HEADS


SMOOTH = 0.1
Z_WEIGHT = 0.0001
CLIP_NORM = 0.08
LEARN_RATE = 100.0
MOMENTUM = 0.5
AVG_DECAY = 0.5
SCORE_SCALE = 0.125
HIDDEN_SCORE = -1e30
EPSILON = 1e-05
HALF_TYPE = jnp.bfloat16
WIDE_NUMBER_TYPE = jnp.float32


def normed(values, gain_row):
    return (
        values * lax.rsqrt(jnp.mean(values * values, axis=-1, keepdims=True) + EPSILON) * gain_row
    )


def rotary(position_row):
    half_dim = HEAD_SIZE // 2
    inv_freq = 10000.0 ** (-jnp.arange(half_dim, dtype=jnp.float32) / half_dim)
    angles = position_row.astype(jnp.float32)[:, None, None] * inv_freq
    return (jnp.cos(angles), jnp.sin(angles))


def rotary_apply(values, cosine_table, sine_values):
    half_dim = HEAD_SIZE // 2
    first_half = values[..., :half_dim]
    second = values[..., half_dim:]
    return jnp.concatenate(
        [
            first_half * cosine_table - second * sine_values,
            second * cosine_table + first_half * sine_values,
        ],
        axis=-1,
    )


def rotate_back(grads_in, cosine_table, sine_values):
    half_dim = HEAD_SIZE // 2
    first_half = grads_in[..., :half_dim]
    second = grads_in[..., half_dim:]
    return jnp.concatenate(
        [
            first_half * cosine_table + second * sine_values,
            second * cosine_table - first_half * sine_values,
        ],
        axis=-1,
    )


def swiglu(gate_up):
    return jax.nn.silu(gate_up[:, :FF]) * gate_up[:, FF:]


def contract(left_side, right_side, left_dim, right_dim):
    return lax.dot_general(
        left_side,
        right_side,
        (((left_dim,), (right_dim,)), ((), ())),
        preferred_element_type=WIDE_NUMBER_TYPE,
    )


def butterfly(values, axis, combine):
    count = lax.axis_size(axis)
    step = 1
    while step < count:
        other = lax.ppermute(values, axis, [(i, i ^ step) for i in range(count)])
        values = combine(values, other)
        step *= 2
    return values


def add_all(values, axes):
    for axis in axes:
        values = butterfly(values, axis, jnp.add)
    return values


def exchange_sum(partial, axis):
    count = lax.axis_size(axis)
    index = lax.axis_index(axis)
    core = index % 2
    place = index // 2
    rows = partial.shape[0] // count
    blocks = partial.reshape(count // 2, 2, rows, partial.shape[1])
    half = lax.dynamic_index_in_dim(blocks, core, axis=1, keepdims=False) + lax.ppermute(
        lax.dynamic_index_in_dim(blocks, 1 - core, axis=1, keepdims=False),
        axis,
        [(i, i ^ 1) for i in range(count)],
    )
    total = lax.dynamic_index_in_dim(half, place, axis=0, keepdims=False)
    for step in range(1, count // 2):
        leaving = lax.dynamic_index_in_dim(half, place ^ step, axis=0, keepdims=False)
        sent = lax.ppermute(
            leaving.astype(HALF_TYPE), axis, [(i, i ^ (2 * step)) for i in range(count)]
        )
        total = total + sent.astype(WIDE_NUMBER_TYPE)
    return total


def window_visible(position_column, key_rows):
    rows = position_column.shape[0]
    base = key_rows - rows
    query_at = lax.broadcasted_iota(jnp.int32, (rows, key_rows), 0) + base
    key_at = lax.broadcasted_iota(jnp.int32, (rows, key_rows), 1)
    return (key_at <= query_at) & (key_at >= query_at - position_column)


def head_slice(head):
    return slice(head * HEAD_SIZE, (head + 1) * HEAD_SIZE)


def attend_kernel(query_ref, key_ref, value_ref, position_ref, out_ref, total_ref):
    key_rows = key_ref.shape[0]
    visible = window_visible(position_ref[...], key_rows)
    for head in range(QUERY_HEADS):
        group = head // GROUPS
        scores = (
            contract(query_ref[:, head_slice(head)], key_ref[:, head_slice(group)], 1, 1)
            * SCORE_SCALE
        )
        scores = jnp.where(visible, scores, HIDDEN_SCORE)
        row_max = jnp.max(scores, axis=1, keepdims=True)
        terms = jnp.exp(scores - row_max)
        row_sum = jnp.sum(terms, axis=1, keepdims=True)
        prob = (terms * (1.0 / row_sum)).astype(HALF_TYPE)
        out_ref[:, head_slice(head)] = contract(
            prob, value_ref[:, head_slice(group)], 1, 0
        ).astype(HALF_TYPE)
        total_ref[:, head : head + 1] = row_max + jnp.log(row_sum)


def attend(query, keys, values, position_column):
    rows = query.shape[0]
    return pl.pallas_call(
        attend_kernel,
        out_shape=(
            jax.ShapeDtypeStruct((rows, QUERY_HEADS * HEAD_SIZE), HALF_TYPE),
            jax.ShapeDtypeStruct((rows, 16), WIDE_NUMBER_TYPE),
        ),
        compiler_params=pltpu.CompilerParams(vmem_limit_bytes=48 << 20),
        name="attend",
    )(query, keys, values, position_column)


def attend_back_kernel(
    query_ref, key_ref, value_ref, total_ref, grad_ref, position_ref, dq_ref, dkv_ref
):
    key_rows = key_ref.shape[0]
    width = KEY_VALUE_HEADS * HEAD_SIZE
    visible = window_visible(position_ref[...], key_rows)
    for group in range(KEY_VALUE_HEADS):
        keys = key_ref[:, head_slice(group)]
        values = value_ref[:, head_slice(group)]
        key_grad = None
        value_grad = None
        for head in range(group * GROUPS, (group + 1) * GROUPS):
            query = query_ref[:, head_slice(head)]
            grad = grad_ref[:, head_slice(head)]
            scores = contract(query, keys, 1, 1) * SCORE_SCALE
            prob = jnp.where(visible, jnp.exp(scores - total_ref[:, head : head + 1]), 0.0)
            grad_prob = contract(grad, values, 1, 1)
            delta = jnp.sum(prob * grad_prob, axis=1, keepdims=True)
            grad_score = (prob * (grad_prob - delta)).astype(HALF_TYPE)
            dq_ref[:, head_slice(head)] = contract(grad_score, keys, 1, 0) * SCORE_SCALE
            key_part = contract(grad_score, query, 0, 0)
            value_part = contract(prob.astype(HALF_TYPE), grad, 0, 0)
            key_grad = key_part if key_grad is None else key_grad + key_part
            value_grad = value_part if value_grad is None else value_grad + value_part
        dkv_ref[:, head_slice(group)] = key_grad * SCORE_SCALE
        dkv_ref[:, width + group * HEAD_SIZE : width + (group + 1) * HEAD_SIZE] = value_grad


def attend_back(query, keys, values, totals, grads, position_column):
    rows = query.shape[0]
    return pl.pallas_call(
        attend_back_kernel,
        out_shape=(
            jax.ShapeDtypeStruct((rows, QUERY_HEADS * HEAD_SIZE), WIDE_NUMBER_TYPE),
            jax.ShapeDtypeStruct(
                (keys.shape[0], 2 * KEY_VALUE_HEADS * HEAD_SIZE), WIDE_NUMBER_TYPE
            ),
        ),
        compiler_params=pltpu.CompilerParams(vmem_limit_bytes=48 << 20),
        name="attend_back",
    )(query, keys, values, totals, grads, position_column)


def stats_kernel(final_ref, target_ref, table_ref, out_ref):
    logits = contract(final_ref[...], table_ref[...], 1, 1)
    row_max = jnp.max(logits, axis=1, keepdims=True)
    exp_sum = jnp.sum(jnp.exp(logits - row_max), axis=1, keepdims=True)
    logit_sum = jnp.sum(logits, axis=1, keepdims=True)
    column = lax.broadcasted_iota(jnp.int32, logits.shape, 1)
    chosen = jnp.sum(jnp.where(column == target_ref[...], logits, 0.0), axis=1, keepdims=True)
    rows = logits.shape[0]
    columns = jnp.concatenate(
        [row_max, exp_sum, logit_sum, chosen, jnp.zeros((rows, 124), WIDE_NUMBER_TYPE)], axis=1
    )
    out_ref[...] = columns.T[:STAT_ROWS]


def combine_kernel(first_ref, second_ref, out_ref):
    joint_max = jnp.maximum(first_ref[0:1], second_ref[0:1])
    out_ref[...] = first_ref[...] + second_ref[...]
    out_ref[0:1] = joint_max
    out_ref[1:2] = first_ref[1:2] * jnp.exp(first_ref[0:1] - joint_max) + second_ref[
        1:2
    ] * jnp.exp(second_ref[0:1] - joint_max)


def combine_stats(first, second):
    return pl.pallas_call(
        combine_kernel,
        out_shape=jax.ShapeDtypeStruct(first.shape, WIDE_NUMBER_TYPE),
        name="combine_stats",
    )(first, second)


STAT_ROWS = 8
TOKEN_TILE = 256


def vocab_stats(finals, target_column, table_rows):
    tokens = finals.shape[0]
    tile = TOKEN_TILE
    return pl.pallas_call(
        stats_kernel,
        grid=(tokens // tile,),
        in_specs=[
            pl.BlockSpec((tile, MODEL_WIDTH), lambda i: (i, 0)),
            pl.BlockSpec((tile, 1), lambda i: (i, 0)),
            pl.BlockSpec(table_rows.shape, lambda i: (0, 0), pipeline_mode=pl.Buffered(1)),
        ],
        out_specs=pl.BlockSpec((STAT_ROWS, tile), lambda i: (0, i)),
        out_shape=jax.ShapeDtypeStruct((STAT_ROWS, tokens), WIDE_NUMBER_TYPE),
        compiler_params=pltpu.CompilerParams(vmem_limit_bytes=56 << 20),
        name="vocab_stats",
    )(finals, target_column, table_rows)


def vocab_grad_kernel(all_tokens, final_ref, target_ref, stat_ref, table_ref, dx_ref, dw_ref):
    finals = final_ref[...]
    table = table_ref[...]
    logits = contract(finals, table, 1, 1)
    lse_row = stat_ref[0:1] + jnp.log(stat_ref[1:2])
    lse = jnp.broadcast_to(lse_row, (128, lse_row.shape[1])).T[:, 0:1]
    column = lax.broadcasted_iota(jnp.int32, logits.shape, 1)
    grad = (
        jnp.exp(logits - lse) * (1.0 + 2.0 * Z_WEIGHT * lse)
        - jnp.where(column == target_ref[...], 1.0 - SMOOTH, 0.0)
        - SMOOTH / V
    ) / all_tokens
    grad = grad.astype(HALF_TYPE)
    dx_ref[...] = contract(grad, table, 1, 0).astype(HALF_TYPE)
    part = contract(grad, finals, 0, 0)

    @pl.when(pl.program_id(0) == 0)
    def _():
        dw_ref[...] = part

    @pl.when(pl.program_id(0) > 0)
    def _():
        dw_ref[...] += part


def vocab_grad(finals, target_column, stats, table_rows, all_tokens):
    tokens = finals.shape[0]
    tile = TOKEN_TILE

    def body(*refs):
        vocab_grad_kernel(all_tokens, *refs)

    return pl.pallas_call(
        body,
        grid=(tokens // tile,),
        in_specs=[
            pl.BlockSpec((tile, MODEL_WIDTH), lambda i: (i, 0)),
            pl.BlockSpec((tile, 1), lambda i: (i, 0)),
            pl.BlockSpec((STAT_ROWS, tile), lambda i: (0, i)),
            pl.BlockSpec(table_rows.shape, lambda i: (0, 0), pipeline_mode=pl.Buffered(1)),
        ],
        out_specs=(
            pl.BlockSpec((tile, MODEL_WIDTH), lambda i: (i, 0)),
            pl.BlockSpec(table_rows.shape, lambda i: (0, 0), pipeline_mode=pl.Buffered(1)),
        ),
        out_shape=(
            jax.ShapeDtypeStruct((tokens, MODEL_WIDTH), HALF_TYPE),
            jax.ShapeDtypeStruct(table_rows.shape, WIDE_NUMBER_TYPE),
        ),
        compiler_params=pltpu.CompilerParams(vmem_limit_bytes=60 << 20),
        name="vocab_grad",
    )(finals, target_column, stats, table_rows)


def advance(weight, grad_one, moment, average, factor):
    clipped = grad_one * factor
    moment_new = MOMENTUM * moment + clipped
    weight_new = weight - LEARN_RATE * (clipped + MOMENTUM * moment_new)
    return (weight_new, moment_new, AVG_DECAY * average + (1.0 - AVG_DECAY) * weight_new)


def shards(
    token_ids,
    targets,
    positions,
    embed_table,
    projection_weight,
    w_out,
    w_gate_up,
    w_down,
    norm_gains,
    table_mom,
    projection_momentum,
    out_mom,
    gate_up_mom,
    down_mom,
    gain_mom,
    table_avg,
    projection_average,
    out_avg,
    gate_up_avg,
    down_avg,
    gain_avg,
):
    ctx_count = lax.axis_size("ctx")
    shard_count = lax.axis_size("shard")
    ctx_index = lax.axis_index("ctx")
    shard_index = lax.axis_index("shard")
    token_rows = token_ids.shape[1]
    own_rows = embed_table.shape[0]
    sequence = token_rows * ctx_count
    all_tokens = sequence * shard_count
    query_span_width = QUERY_HEADS * HEAD_SIZE
    key_value_width = KEY_VALUE_HEADS * HEAD_SIZE
    back = ctx_count // 2

    table_rows = lax.all_gather(embed_table.astype(HALF_TYPE), "shard", axis=0, tiled=True)
    slice_rows = table_rows.shape[0]
    pairs = lax.all_gather(
        jnp.concatenate([token_ids, targets], axis=0), ("ctx", "shard"), axis=0
    ).reshape(ctx_count, shard_count, 2, token_rows)
    sequence_pairs = lax.dynamic_index_in_dim(pairs, shard_index, axis=1, keepdims=False)
    first_row = ctx_index * slice_rows
    id_row = sequence_pairs[:, 0].reshape(sequence) - first_row
    target_column = sequence_pairs[:, 1].reshape(sequence, 1) - first_row
    id_here = (id_row >= 0) & (id_row < slice_rows)
    picked = jnp.where(
        id_here[:, None], table_rows[jnp.where(id_here, id_row, 0)], jnp.zeros((), HALF_TYPE)
    )
    looked_up = lax.all_to_all(
        picked.reshape(ctx_count, token_rows, MODEL_WIDTH), "ctx", 0, 0, tiled=True
    )
    hidden = jnp.sum(looked_up.astype(WIDE_NUMBER_TYPE), axis=0)
    position_row = positions[0]
    position_column = position_row[:, None]
    cosine_table, sine_values = rotary(position_row)
    gain_values = lax.all_gather(
        norm_gains.astype(HALF_TYPE), "shard", axis=1, tiled=True
    ).astype(WIDE_NUMBER_TYPE)

    def gathered(weight, layer_id):
        return lax.all_gather(weight[layer_id].astype(HALF_TYPE), "shard", axis=0, tiled=True)

    fetched = [
        tuple(gathered(weight, layer_id) for weight in (projection_weight, w_out, w_gate_up, w_down))
        for layer_id in range(LAYER_COUNT)
    ]

    saved_state = []
    for layer_id in range(LAYER_COUNT):
        qkv_full, out_full, gate_up_full, down_full = fetched[layer_id]
        layer_input = hidden
        attn_in = normed(hidden, gain_values[2 * layer_id]).astype(HALF_TYPE)
        projected_kv = jnp.dot(
            attn_in, qkv_full[:, query_span_width:], preferred_element_type=WIDE_NUMBER_TYPE
        )
        key_rows = (
            rotary_apply(
                projected_kv[:, :key_value_width].reshape(token_rows, KEY_VALUE_HEADS, HEAD_SIZE),
                cosine_table,
                sine_values,
            )
            .astype(HALF_TYPE)
            .reshape(token_rows, key_value_width)
        )
        own_kv = jnp.concatenate(
            [key_rows, projected_kv[:, key_value_width:].astype(HALF_TYPE)], axis=1
        )
        window = [
            lax.ppermute(own_kv, "ctx", [(i, i + step) for i in range(ctx_count - step)])
            for step in range(back, 0, -1)
        ]
        window_kv = jnp.concatenate(window + [own_kv], axis=0)
        window_keys = window_kv[:, :key_value_width]
        window_values = window_kv[:, key_value_width:]
        projected_query = jnp.dot(
            attn_in, qkv_full[:, :query_span_width], preferred_element_type=WIDE_NUMBER_TYPE
        )
        query = (
            rotary_apply(
                projected_query.reshape(token_rows, QUERY_HEADS, HEAD_SIZE),
                cosine_table,
                sine_values,
            )
            .astype(HALF_TYPE)
            .reshape(token_rows, query_span_width)
        )
        attn_out, log_total = attend(query, window_keys, window_values, position_column)
        hidden = hidden + jnp.dot(attn_out, out_full, preferred_element_type=WIDE_NUMBER_TYPE)
        middle = hidden
        mlp_in = normed(hidden, gain_values[2 * layer_id + 1]).astype(HALF_TYPE)
        gate_up = jnp.dot(mlp_in, gate_up_full, preferred_element_type=WIDE_NUMBER_TYPE)
        act_half = swiglu(gate_up).astype(HALF_TYPE)
        hidden = hidden + jnp.dot(act_half, down_full, preferred_element_type=WIDE_NUMBER_TYPE)
        saved_state.append(
            (
                layer_input,
                middle,
                query,
                window_keys,
                window_values,
                log_total,
                attn_out,
                attn_in,
                mlp_in,
                gate_up,
                act_half,
            )
        )
    final_gain = gain_values[2 * LAYER_COUNT]
    final_half = normed(hidden, final_gain).astype(HALF_TYPE)
    sequence_final = lax.all_gather(final_half, "ctx", axis=0, tiled=True)

    stats = vocab_stats(sequence_final, target_column, table_rows)
    stats = butterfly(stats, "ctx", combine_stats)
    hidden_grad_parts, slice_grad = vocab_grad(
        sequence_final, target_column, stats, table_rows, all_tokens
    )
    row_lse = stats[0] + jnp.log(stats[1])
    token_loss = (
        row_lse
        - (1.0 - SMOOTH) * stats[3]
        - SMOOTH * stats[2] / V
        + Z_WEIGHT * row_lse * row_lse
    )
    own_loss = (
        jnp.sum(lax.dynamic_slice_in_dim(token_loss, ctx_index * token_rows, token_rows))
        / all_tokens
    )
    hidden_grad = jnp.sum(
        lax.all_to_all(
            hidden_grad_parts.reshape(ctx_count, token_rows, MODEL_WIDTH), "ctx", 0, 0, tiled=True
        ).astype(WIDE_NUMBER_TYPE),
        axis=0,
    )
    _, final_back = jax.vjp(normed, hidden, final_gain)
    grad_hidden, grad_final_gain = final_back(hidden_grad)
    layer_grads = [None] * LAYER_COUNT
    gain_rows = [None] * (2 * LAYER_COUNT) + [grad_final_gain]
    for layer_id in reversed(range(LAYER_COUNT)):
        (
            layer_input,
            middle,
            query,
            window_keys,
            window_values,
            log_total,
            attn_out,
            attn_in,
            mlp_in,
            gate_up,
            act_half,
        ) = saved_state[layer_id]
        qkv_full, out_full, gate_up_full, down_full = fetched[layer_id]
        _, mlp_back = jax.vjp(normed, middle, gain_values[2 * layer_id + 1])
        _, act_back = jax.vjp(swiglu, gate_up)
        out_grad = grad_hidden.astype(HALF_TYPE)
        grad_down = contract(act_half, out_grad, 0, 0)
        grad_act = contract(out_grad, down_full, 1, 1)
        grad_gate_up = act_back(grad_act)[0].astype(HALF_TYPE)
        grad_gu_weight = contract(mlp_in, grad_gate_up, 0, 0)
        grad_middle, gain_rows[2 * layer_id + 1] = mlp_back(
            contract(grad_gate_up, gate_up_full, 1, 1)
        )
        grad_hidden = grad_hidden + grad_middle
        branch_grad = grad_hidden.astype(HALF_TYPE)
        grad_out_weight = contract(attn_out, branch_grad, 0, 0)
        grad_attended = contract(branch_grad, out_full, 1, 1).astype(HALF_TYPE)
        if layer_id < LAYER_COUNT - 1:
            above = layer_grads[layer_id + 1]
            grad_attended, above_mlp = lax.optimization_barrier((grad_attended, above[2:]))
            layer_grads[layer_id + 1] = above[:2] + above_mlp
        mlp_grads = tuple(
            exchange_sum(partial, "shard") for partial in (grad_gu_weight, grad_down)
        )
        query_gradient, window_grad = attend_back(
            query, window_keys, window_values, log_total, grad_attended, position_column
        )
        key_value_gradient = window_grad[back * token_rows :]
        for step in range(1, back + 1):
            part = window_grad[(back - step) * token_rows : (back - step + 1) * token_rows]
            key_value_gradient = key_value_gradient + lax.ppermute(
                part.astype(HALF_TYPE), "ctx", [(i + step, i) for i in range(ctx_count - step)]
            ).astype(WIDE_NUMBER_TYPE)
        _, attn_back = jax.vjp(normed, layer_input, gain_values[2 * layer_id])
        grad_projected = jnp.concatenate(
            [
                rotate_back(
                    query_gradient.reshape(token_rows, QUERY_HEADS, HEAD_SIZE),
                    cosine_table,
                    sine_values,
                ).reshape(token_rows, query_span_width),
                rotate_back(
                    key_value_gradient[:, :key_value_width].reshape(
                        token_rows, KEY_VALUE_HEADS, HEAD_SIZE
                    ),
                    cosine_table,
                    sine_values,
                ).reshape(token_rows, key_value_width),
                key_value_gradient[:, key_value_width:],
            ],
            axis=1,
        ).astype(HALF_TYPE)
        grad_qkv_weight = contract(attn_in, grad_projected, 0, 0)
        grad_input, gain_rows[2 * layer_id] = attn_back(contract(grad_projected, qkv_full, 1, 1))
        grad_hidden = grad_hidden + grad_input
        attn_grads = tuple(
            exchange_sum(partial, "shard") for partial in (grad_qkv_weight, grad_out_weight)
        )
        layer_grads[layer_id] = attn_grads + mlp_grads
    sequence_grad = lax.all_gather(grad_hidden.astype(HALF_TYPE), "ctx", axis=0, tiled=True)
    last = LAYER_COUNT - 1
    early = lax.psum(layer_grads[last][2:], "ctx")
    late = tuple(layer_grads[:last]) + (layer_grads[last][:2],)
    early, late = lax.optimization_barrier((early, late))
    late = lax.psum(late, "ctx")
    layer_grads = list(late[:last]) + [late[last] + early]
    chosen_rows = jnp.arange(slice_rows)[:, None] == id_row[None, :]
    table_grad = exchange_sum(
        slice_grad + contract(chosen_rows.astype(HALF_TYPE), sequence_grad, 1, 0), "shard"
    )
    gain_total = add_all(jnp.stack(gain_rows), ("ctx", "shard"))
    gain_width = norm_gains.shape[1]
    gain_grad = lax.dynamic_slice_in_dim(gain_total, shard_index * gain_width, gain_width, axis=1)
    qkv_grad, out_grad_all, gate_up_grad, down_grad = [
        jnp.stack([layer_grads[layer_no][which] for layer_no in range(LAYER_COUNT)])
        for which in range(4)
    ]
    layer_square = sum(
        (
            jnp.sum(grad_one * grad_one)
            for grad_one in (qkv_grad, out_grad_all, gate_up_grad, down_grad, gain_grad)
        )
    )
    sums = add_all(
        jnp.stack([own_loss, layer_square / ctx_count + jnp.sum(table_grad * table_grad)]),
        ("ctx", "shard"),
    )
    loss_sum, square_sum = sums[0], sums[1]
    grad_norm = jnp.sqrt(square_sum)
    factor = CLIP_NORM / jnp.maximum(grad_norm, CLIP_NORM)
    table_new = advance(embed_table, table_grad, table_mom, table_avg, factor)
    qkv_new = advance(projection_weight, qkv_grad, projection_momentum, projection_average, factor)
    out_new = advance(w_out, out_grad_all, out_mom, out_avg, factor)
    gate_up_new = advance(w_gate_up, gate_up_grad, gate_up_mom, gate_up_avg, factor)
    down_new = advance(w_down, down_grad, down_mom, down_avg, factor)
    gains_new = advance(norm_gains, gain_grad, gain_mom, gain_avg, factor)
    return (
        loss_sum,
        grad_norm,
        table_new[0],
        qkv_new[0],
        out_new[0],
        gate_up_new[0],
        down_new[0],
        gains_new[0],
        table_new[1],
        qkv_new[1],
        out_new[1],
        gate_up_new[1],
        down_new[1],
        gains_new[1],
        table_new[2],
        qkv_new[2],
        out_new[2],
        gate_up_new[2],
        down_new[2],
        gains_new[2],
    )


def solution(mesh):
    return jax.shard_map(
        shards,
        mesh=mesh,
        in_specs=(
            P("shard", "ctx"),
            P("shard", "ctx"),
            P("shard", "ctx"),
            P(("ctx", "shard"), None),
            P(None, "shard", None),
            P(None, "shard", None),
            P(None, "shard", None),
            P(None, "shard", None),
            P(None, "shard"),
            P(("ctx", "shard"), None),
            P(None, "shard", None),
            P(None, "shard", None),
            P(None, "shard", None),
            P(None, "shard", None),
            P(None, "shard"),
            P(("ctx", "shard"), None),
            P(None, "shard", None),
            P(None, "shard", None),
            P(None, "shard", None),
            P(None, "shard", None),
            P(None, "shard"),
        ),
        out_specs=(
            P(),
            P(),
            P(("ctx", "shard"), None),
            P(None, "shard", None),
            P(None, "shard", None),
            P(None, "shard", None),
            P(None, "shard", None),
            P(None, "shard"),
            P(("ctx", "shard"), None),
            P(None, "shard", None),
            P(None, "shard", None),
            P(None, "shard", None),
            P(None, "shard", None),
            P(None, "shard"),
            P(("ctx", "shard"), None),
            P(None, "shard", None),
            P(None, "shard", None),
            P(None, "shard", None),
            P(None, "shard", None),
            P(None, "shard"),
        ),
        check_vma=False,
    )
```

```python
import jax
import jax.numpy as jnp
from jax import lax
from jax.experimental import pallas as pl
from jax.experimental.pallas import tpu as pltpu
from jax.sharding import PartitionSpec as P

MODEL_WIDTH = 576
QUERY_HEADS = 9
KEY_VALUE_HEADS = 3
HEAD_SIZE = 64
FF = 1536
V = 32000
LAYER_COUNT = 2
GROUPS = QUERY_HEADS // KEY_VALUE_HEADS


SMOOTH = 0.1
Z_WEIGHT = 0.0001
CLIP_NORM = 0.08
LEARN_RATE = 100.0
MOMENTUM = 0.5
AVG_DECAY = 0.5
SCORE_SCALE = 0.125
HIDDEN_SCORE = -1e30
EPSILON = 1e-05
HALF_TYPE = jnp.bfloat16
WIDE_NUMBER_TYPE = jnp.float32


def normed(values, gain_row):
    return (
        values * lax.rsqrt(jnp.mean(values * values, axis=-1, keepdims=True) + EPSILON) * gain_row
    )


def rotary(position_row):
    half_dim = HEAD_SIZE // 2
    inv_freq = 10000.0 ** (-jnp.arange(half_dim, dtype=jnp.float32) / half_dim)
    angles = position_row.astype(jnp.float32)[:, None, None] * inv_freq
    return (jnp.cos(angles), jnp.sin(angles))


def rotary_apply(values, cosine_table, sine_values):
    half_dim = HEAD_SIZE // 2
    first_half = values[..., :half_dim]
    second = values[..., half_dim:]
    return jnp.concatenate(
        [
            first_half * cosine_table - second * sine_values,
            second * cosine_table + first_half * sine_values,
        ],
        axis=-1,
    )


def rotate_back(grads_in, cosine_table, sine_values):
    half_dim = HEAD_SIZE // 2
    first_half = grads_in[..., :half_dim]
    second = grads_in[..., half_dim:]
    return jnp.concatenate(
        [
            first_half * cosine_table + second * sine_values,
            second * cosine_table - first_half * sine_values,
        ],
        axis=-1,
    )


def swiglu(gate_up):
    return jax.nn.silu(gate_up[:, :FF]) * gate_up[:, FF:]


def contract(left_side, right_side, left_dim, right_dim):
    return lax.dot_general(
        left_side,
        right_side,
        (((left_dim,), (right_dim,)), ((), ())),
        preferred_element_type=WIDE_NUMBER_TYPE,
    )


def butterfly(values, axis, combine):
    count = lax.axis_size(axis)
    step = 1
    while step < count:
        other = lax.ppermute(values, axis, [(i, i ^ step) for i in range(count)])
        values = combine(values, other)
        step *= 2
    return values


def add_all(values, axes):
    for axis in axes:
        values = butterfly(values, axis, jnp.add)
    return values


def exchange_halves(half_of, axis):
    count = lax.axis_size(axis)
    index = lax.axis_index(axis)
    core = index % 2
    place = index // 2
    leaving = half_of(1 - core)
    half = half_of(core) + lax.ppermute(leaving, axis, [(i, i ^ 1) for i in range(count)])
    half = half.reshape(count // 2, half.shape[0] // (count // 2), half.shape[1])
    total = lax.dynamic_index_in_dim(half, place, axis=0, keepdims=False)
    for step in range(1, count // 2):
        leaving = lax.dynamic_index_in_dim(half, place ^ step, axis=0, keepdims=False)
        sent = lax.ppermute(
            leaving.astype(HALF_TYPE), axis, [(i, i ^ (2 * step)) for i in range(count)]
        )
        total = total + sent.astype(WIDE_NUMBER_TYPE)
    return total


def exchange_sum(partial, axis):
    count = lax.axis_size(axis)
    blocks = partial.reshape(count // 2, 2, partial.shape[0] // count, partial.shape[1])

    def half_of(core):
        half = lax.dynamic_index_in_dim(blocks, core, axis=1, keepdims=False)
        return half.reshape(partial.shape[0] // 2, partial.shape[1])

    return exchange_halves(half_of, axis)


def exchange_product(left_side, right_side, axis):
    count = lax.axis_size(axis)
    tokens, width = left_side.shape
    columns = left_side.reshape(tokens, count // 2, 2, width // count)

    def half_of(core):
        chosen = lax.dynamic_index_in_dim(columns, core, axis=2, keepdims=False)
        return contract(chosen.reshape(tokens, width // 2), right_side, 0, 0)

    return exchange_halves(half_of, axis)


def window_visible(position_column, key_rows):
    rows = position_column.shape[0]
    base = key_rows - rows
    query_at = lax.broadcasted_iota(jnp.int32, (rows, key_rows), 0) + base
    key_at = lax.broadcasted_iota(jnp.int32, (rows, key_rows), 1)
    return (key_at <= query_at) & (key_at >= query_at - position_column)


def head_slice(head):
    return slice(head * HEAD_SIZE, (head + 1) * HEAD_SIZE)


def attend_kernel(query_ref, key_ref, value_ref, position_ref, out_ref, total_ref):
    key_rows = key_ref.shape[0]
    visible = window_visible(position_ref[...], key_rows)
    for head in range(QUERY_HEADS):
        group = head // GROUPS
        scores = (
            contract(query_ref[:, head_slice(head)], key_ref[:, head_slice(group)], 1, 1)
            * SCORE_SCALE
        )
        scores = jnp.where(visible, scores, HIDDEN_SCORE)
        row_max = jnp.max(scores, axis=1, keepdims=True)
        terms = jnp.exp(scores - row_max)
        row_sum = jnp.sum(terms, axis=1, keepdims=True)
        prob = (terms * (1.0 / row_sum)).astype(HALF_TYPE)
        out_ref[:, head_slice(head)] = contract(
            prob, value_ref[:, head_slice(group)], 1, 0
        ).astype(HALF_TYPE)
        total_ref[:, head : head + 1] = row_max + jnp.log(row_sum)


def attend(query, keys, values, position_column):
    rows = query.shape[0]
    return pl.pallas_call(
        attend_kernel,
        out_shape=(
            jax.ShapeDtypeStruct((rows, QUERY_HEADS * HEAD_SIZE), HALF_TYPE),
            jax.ShapeDtypeStruct((rows, 16), WIDE_NUMBER_TYPE),
        ),
        compiler_params=pltpu.CompilerParams(vmem_limit_bytes=48 << 20),
        name="attend",
    )(query, keys, values, position_column)


def attend_back_kernel(
    query_ref, key_ref, value_ref, total_ref, grad_ref, position_ref, dq_ref, dkv_ref
):
    key_rows = key_ref.shape[0]
    width = KEY_VALUE_HEADS * HEAD_SIZE
    visible = window_visible(position_ref[...], key_rows)
    for group in range(KEY_VALUE_HEADS):
        keys = key_ref[:, head_slice(group)]
        values = value_ref[:, head_slice(group)]
        key_grad = None
        value_grad = None
        for head in range(group * GROUPS, (group + 1) * GROUPS):
            query = query_ref[:, head_slice(head)]
            grad = grad_ref[:, head_slice(head)]
            scores = contract(query, keys, 1, 1) * SCORE_SCALE
            prob = jnp.where(visible, jnp.exp(scores - total_ref[:, head : head + 1]), 0.0)
            grad_prob = contract(grad, values, 1, 1)
            delta = jnp.sum(prob * grad_prob, axis=1, keepdims=True)
            grad_score = (prob * (grad_prob - delta)).astype(HALF_TYPE)
            dq_ref[:, head_slice(head)] = contract(grad_score, keys, 1, 0) * SCORE_SCALE
            key_part = contract(grad_score, query, 0, 0)
            value_part = contract(prob.astype(HALF_TYPE), grad, 0, 0)
            key_grad = key_part if key_grad is None else key_grad + key_part
            value_grad = value_part if value_grad is None else value_grad + value_part
        dkv_ref[:, head_slice(group)] = key_grad * SCORE_SCALE
        dkv_ref[:, width + group * HEAD_SIZE : width + (group + 1) * HEAD_SIZE] = value_grad


def attend_back(query, keys, values, totals, grads, position_column):
    rows = query.shape[0]
    return pl.pallas_call(
        attend_back_kernel,
        out_shape=(
            jax.ShapeDtypeStruct((rows, QUERY_HEADS * HEAD_SIZE), WIDE_NUMBER_TYPE),
            jax.ShapeDtypeStruct(
                (keys.shape[0], 2 * KEY_VALUE_HEADS * HEAD_SIZE), WIDE_NUMBER_TYPE
            ),
        ),
        compiler_params=pltpu.CompilerParams(vmem_limit_bytes=48 << 20),
        name="attend_back",
    )(query, keys, values, totals, grads, position_column)


def stats_kernel(final_ref, target_ref, table_ref, out_ref):
    logits = contract(final_ref[...], table_ref[...], 1, 1)
    row_max = jnp.max(logits, axis=1, keepdims=True)
    exp_sum = jnp.sum(jnp.exp(logits - row_max), axis=1, keepdims=True)
    logit_sum = jnp.sum(logits, axis=1, keepdims=True)
    column = lax.broadcasted_iota(jnp.int32, logits.shape, 1)
    chosen = jnp.sum(jnp.where(column == target_ref[...], logits, 0.0), axis=1, keepdims=True)
    rows = logits.shape[0]
    columns = jnp.concatenate(
        [row_max, exp_sum, logit_sum, chosen, jnp.zeros((rows, 124), WIDE_NUMBER_TYPE)], axis=1
    )
    out_ref[...] = columns.T[:STAT_ROWS]


def combine_kernel(first_ref, second_ref, out_ref):
    joint_max = jnp.maximum(first_ref[0:1], second_ref[0:1])
    out_ref[...] = first_ref[...] + second_ref[...]
    out_ref[0:1] = joint_max
    out_ref[1:2] = first_ref[1:2] * jnp.exp(first_ref[0:1] - joint_max) + second_ref[
        1:2
    ] * jnp.exp(second_ref[0:1] - joint_max)


def combine_stats(first, second):
    return pl.pallas_call(
        combine_kernel,
        out_shape=jax.ShapeDtypeStruct(first.shape, WIDE_NUMBER_TYPE),
        name="combine_stats",
    )(first, second)


STAT_ROWS = 8
TOKEN_TILE = 256


def vocab_stats(finals, target_column, table_rows):
    tokens = finals.shape[0]
    tile = TOKEN_TILE
    return pl.pallas_call(
        stats_kernel,
        grid=(tokens // tile,),
        in_specs=[
            pl.BlockSpec((tile, MODEL_WIDTH), lambda i: (i, 0)),
            pl.BlockSpec((tile, 1), lambda i: (i, 0)),
            pl.BlockSpec(table_rows.shape, lambda i: (0, 0), pipeline_mode=pl.Buffered(1)),
        ],
        out_specs=pl.BlockSpec((STAT_ROWS, tile), lambda i: (0, i)),
        out_shape=jax.ShapeDtypeStruct((STAT_ROWS, tokens), WIDE_NUMBER_TYPE),
        compiler_params=pltpu.CompilerParams(vmem_limit_bytes=56 << 20),
        name="vocab_stats",
    )(finals, target_column, table_rows)


def vocab_grad_kernel(all_tokens, final_ref, target_ref, stat_ref, table_ref, dx_ref, dw_ref):
    finals = final_ref[...]
    table = table_ref[...]
    logits = contract(finals, table, 1, 1)
    lse_row = stat_ref[0:1] + jnp.log(stat_ref[1:2])
    lse = jnp.broadcast_to(lse_row, (128, lse_row.shape[1])).T[:, 0:1]
    column = lax.broadcasted_iota(jnp.int32, logits.shape, 1)
    grad = (
        jnp.exp(logits - lse) * (1.0 + 2.0 * Z_WEIGHT * lse)
        - jnp.where(column == target_ref[...], 1.0 - SMOOTH, 0.0)
        - SMOOTH / V
    ) / all_tokens
    grad = grad.astype(HALF_TYPE)
    dx_ref[...] = contract(grad, table, 1, 0).astype(HALF_TYPE)
    part = contract(grad, finals, 0, 0)

    @pl.when(pl.program_id(0) == 0)
    def _():
        dw_ref[...] = part

    @pl.when(pl.program_id(0) > 0)
    def _():
        dw_ref[...] += part


def vocab_grad(finals, target_column, stats, table_rows, all_tokens):
    tokens = finals.shape[0]
    tile = TOKEN_TILE

    def body(*refs):
        vocab_grad_kernel(all_tokens, *refs)

    return pl.pallas_call(
        body,
        grid=(tokens // tile,),
        in_specs=[
            pl.BlockSpec((tile, MODEL_WIDTH), lambda i: (i, 0)),
            pl.BlockSpec((tile, 1), lambda i: (i, 0)),
            pl.BlockSpec((STAT_ROWS, tile), lambda i: (0, i)),
            pl.BlockSpec(table_rows.shape, lambda i: (0, 0), pipeline_mode=pl.Buffered(1)),
        ],
        out_specs=(
            pl.BlockSpec((tile, MODEL_WIDTH), lambda i: (i, 0)),
            pl.BlockSpec(table_rows.shape, lambda i: (0, 0), pipeline_mode=pl.Buffered(1)),
        ),
        out_shape=(
            jax.ShapeDtypeStruct((tokens, MODEL_WIDTH), HALF_TYPE),
            jax.ShapeDtypeStruct(table_rows.shape, WIDE_NUMBER_TYPE),
        ),
        compiler_params=pltpu.CompilerParams(vmem_limit_bytes=60 << 20),
        name="vocab_grad",
    )(finals, target_column, stats, table_rows)


def advance(weight, grad_one, moment, average, factor):
    clipped = grad_one * factor
    moment_new = MOMENTUM * moment + clipped
    weight_new = weight - LEARN_RATE * (clipped + MOMENTUM * moment_new)
    return (weight_new, moment_new, AVG_DECAY * average + (1.0 - AVG_DECAY) * weight_new)


def shards(
    token_ids,
    targets,
    positions,
    embed_table,
    projection_weight,
    w_out,
    w_gate_up,
    w_down,
    norm_gains,
    table_mom,
    projection_momentum,
    out_mom,
    gate_up_mom,
    down_mom,
    gain_mom,
    table_avg,
    projection_average,
    out_avg,
    gate_up_avg,
    down_avg,
    gain_avg,
):
    ctx_count = lax.axis_size("ctx")
    shard_count = lax.axis_size("shard")
    ctx_index = lax.axis_index("ctx")
    shard_index = lax.axis_index("shard")
    token_rows = token_ids.shape[1]
    own_rows = embed_table.shape[0]
    sequence = token_rows * ctx_count
    all_tokens = sequence * shard_count
    query_span_width = QUERY_HEADS * HEAD_SIZE
    key_value_width = KEY_VALUE_HEADS * HEAD_SIZE
    back = ctx_count // 2

    table_rows = lax.all_gather(embed_table.astype(HALF_TYPE), "shard", axis=0, tiled=True)
    slice_rows = table_rows.shape[0]
    pairs = lax.all_gather(
        jnp.concatenate([token_ids, targets], axis=0), ("ctx", "shard"), axis=0
    ).reshape(ctx_count, shard_count, 2, token_rows)
    sequence_pairs = lax.dynamic_index_in_dim(pairs, shard_index, axis=1, keepdims=False)
    first_row = ctx_index * slice_rows
    id_row = sequence_pairs[:, 0].reshape(sequence) - first_row
    target_column = sequence_pairs[:, 1].reshape(sequence, 1) - first_row
    id_here = (id_row >= 0) & (id_row < slice_rows)
    picked = jnp.where(
        id_here[:, None], table_rows[jnp.where(id_here, id_row, 0)], jnp.zeros((), HALF_TYPE)
    )
    looked_up = lax.all_to_all(
        picked.reshape(ctx_count, token_rows, MODEL_WIDTH), "ctx", 0, 0, tiled=True
    )
    hidden = jnp.sum(looked_up.astype(WIDE_NUMBER_TYPE), axis=0)
    position_row = positions[0]
    position_column = position_row[:, None]
    cosine_table, sine_values = rotary(position_row)
    gain_values = lax.all_gather(
        norm_gains.astype(HALF_TYPE), "shard", axis=1, tiled=True
    ).astype(WIDE_NUMBER_TYPE)

    def gathered(weight, layer_id):
        return lax.all_gather(weight[layer_id].astype(HALF_TYPE), "shard", axis=0, tiled=True)

    fetched = [
        tuple(gathered(weight, layer_id) for weight in (projection_weight, w_out, w_gate_up, w_down))
        for layer_id in range(LAYER_COUNT)
    ]

    saved_state = []
    for layer_id in range(LAYER_COUNT):
        qkv_full, out_full, gate_up_full, down_full = fetched[layer_id]
        layer_input = hidden
        attn_in = normed(hidden, gain_values[2 * layer_id]).astype(HALF_TYPE)
        projected_kv = jnp.dot(
            attn_in, qkv_full[:, query_span_width:], preferred_element_type=WIDE_NUMBER_TYPE
        )
        key_rows = (
            rotary_apply(
                projected_kv[:, :key_value_width].reshape(token_rows, KEY_VALUE_HEADS, HEAD_SIZE),
                cosine_table,
                sine_values,
            )
            .astype(HALF_TYPE)
            .reshape(token_rows, key_value_width)
        )
        own_kv = jnp.concatenate(
            [key_rows, projected_kv[:, key_value_width:].astype(HALF_TYPE)], axis=1
        )
        window = [
            lax.ppermute(own_kv, "ctx", [(i, i + step) for i in range(ctx_count - step)])
            for step in range(back, 0, -1)
        ]
        window_kv = jnp.concatenate(window + [own_kv], axis=0)
        window_keys = window_kv[:, :key_value_width]
        window_values = window_kv[:, key_value_width:]
        projected_query = jnp.dot(
            attn_in, qkv_full[:, :query_span_width], preferred_element_type=WIDE_NUMBER_TYPE
        )
        query = (
            rotary_apply(
                projected_query.reshape(token_rows, QUERY_HEADS, HEAD_SIZE),
                cosine_table,
                sine_values,
            )
            .astype(HALF_TYPE)
            .reshape(token_rows, query_span_width)
        )
        attn_out, log_total = attend(query, window_keys, window_values, position_column)
        hidden = hidden + jnp.dot(attn_out, out_full, preferred_element_type=WIDE_NUMBER_TYPE)
        middle = hidden
        mlp_in = normed(hidden, gain_values[2 * layer_id + 1]).astype(HALF_TYPE)
        gate_up = jnp.dot(mlp_in, gate_up_full, preferred_element_type=WIDE_NUMBER_TYPE)
        act_half = swiglu(gate_up).astype(HALF_TYPE)
        hidden = hidden + jnp.dot(act_half, down_full, preferred_element_type=WIDE_NUMBER_TYPE)
        saved_state.append(
            (
                layer_input,
                middle,
                query,
                window_keys,
                window_values,
                log_total,
                attn_out,
                attn_in,
                mlp_in,
                gate_up,
                act_half,
            )
        )
    final_gain = gain_values[2 * LAYER_COUNT]
    final_half = normed(hidden, final_gain).astype(HALF_TYPE)
    sequence_final = lax.all_gather(final_half, "ctx", axis=0, tiled=True)

    stats = vocab_stats(sequence_final, target_column, table_rows)
    stats = butterfly(stats, "ctx", combine_stats)
    hidden_grad_parts, slice_grad = vocab_grad(
        sequence_final, target_column, stats, table_rows, all_tokens
    )
    row_lse = stats[0] + jnp.log(stats[1])
    token_loss = (
        row_lse
        - (1.0 - SMOOTH) * stats[3]
        - SMOOTH * stats[2] / V
        + Z_WEIGHT * row_lse * row_lse
    )
    own_loss = (
        jnp.sum(lax.dynamic_slice_in_dim(token_loss, ctx_index * token_rows, token_rows))
        / all_tokens
    )
    hidden_grad = jnp.sum(
        lax.all_to_all(
            hidden_grad_parts.reshape(ctx_count, token_rows, MODEL_WIDTH), "ctx", 0, 0, tiled=True
        ).astype(WIDE_NUMBER_TYPE),
        axis=0,
    )
    _, final_back = jax.vjp(normed, hidden, final_gain)
    grad_hidden, grad_final_gain = final_back(hidden_grad)
    layer_grads = [None] * LAYER_COUNT
    gain_rows = [None] * (2 * LAYER_COUNT) + [grad_final_gain]
    for layer_id in reversed(range(LAYER_COUNT)):
        (
            layer_input,
            middle,
            query,
            window_keys,
            window_values,
            log_total,
            attn_out,
            attn_in,
            mlp_in,
            gate_up,
            act_half,
        ) = saved_state[layer_id]
        qkv_full, out_full, gate_up_full, down_full = fetched[layer_id]
        _, mlp_back = jax.vjp(normed, middle, gain_values[2 * layer_id + 1])
        _, act_back = jax.vjp(swiglu, gate_up)
        out_grad = grad_hidden.astype(HALF_TYPE)
        grad_act = contract(out_grad, down_full, 1, 1)
        grad_gate_up = act_back(grad_act)[0].astype(HALF_TYPE)
        grad_middle, gain_rows[2 * layer_id + 1] = mlp_back(
            contract(grad_gate_up, gate_up_full, 1, 1)
        )
        grad_hidden = grad_hidden + grad_middle
        branch_grad = grad_hidden.astype(HALF_TYPE)
        grad_attended = contract(branch_grad, out_full, 1, 1).astype(HALF_TYPE)
        mlp_grads = (
            exchange_product(mlp_in, grad_gate_up, "shard"),
            exchange_product(act_half, out_grad, "shard"),
        )
        query_gradient, window_grad = attend_back(
            query, window_keys, window_values, log_total, grad_attended, position_column
        )
        key_value_gradient = window_grad[back * token_rows :]
        for step in range(1, back + 1):
            part = window_grad[(back - step) * token_rows : (back - step + 1) * token_rows]
            key_value_gradient = key_value_gradient + lax.ppermute(
                part.astype(HALF_TYPE), "ctx", [(i + step, i) for i in range(ctx_count - step)]
            ).astype(WIDE_NUMBER_TYPE)
        if layer_id > 0:
            mlp_grads, key_value_gradient = lax.optimization_barrier(
                (mlp_grads, key_value_gradient)
            )
        _, attn_back = jax.vjp(normed, layer_input, gain_values[2 * layer_id])
        grad_projected = jnp.concatenate(
            [
                rotate_back(
                    query_gradient.reshape(token_rows, QUERY_HEADS, HEAD_SIZE),
                    cosine_table,
                    sine_values,
                ).reshape(token_rows, query_span_width),
                rotate_back(
                    key_value_gradient[:, :key_value_width].reshape(
                        token_rows, KEY_VALUE_HEADS, HEAD_SIZE
                    ),
                    cosine_table,
                    sine_values,
                ).reshape(token_rows, key_value_width),
                key_value_gradient[:, key_value_width:],
            ],
            axis=1,
        ).astype(HALF_TYPE)
        grad_input, gain_rows[2 * layer_id] = attn_back(contract(grad_projected, qkv_full, 1, 1))
        grad_hidden = grad_hidden + grad_input
        attn_grads = (
            exchange_product(attn_in, grad_projected, "shard"),
            exchange_product(attn_out, branch_grad, "shard"),
        )
        layer_grads[layer_id] = attn_grads + mlp_grads
    copies = jnp.broadcast_to(
        grad_hidden.astype(HALF_TYPE)[None], (ctx_count, token_rows, MODEL_WIDTH)
    )
    sequence_grad = lax.all_to_all(copies, "ctx", 0, 0, tiled=True).reshape(sequence, MODEL_WIDTH)
    last = LAYER_COUNT - 1
    early = lax.psum(layer_grads[last][2:], "ctx")
    late = tuple(layer_grads[:last]) + (layer_grads[last][:2],)
    early, late = lax.optimization_barrier((early, late))
    late = lax.psum(late, "ctx")
    layer_grads = list(late[:last]) + [late[last] + early]
    chosen_rows = jnp.arange(slice_rows)[:, None] == id_row[None, :]
    table_grad = exchange_sum(
        slice_grad + contract(chosen_rows.astype(HALF_TYPE), sequence_grad, 1, 0), "shard"
    )
    gain_total = add_all(jnp.stack(gain_rows), ("ctx", "shard"))
    gain_width = norm_gains.shape[1]
    gain_grad = lax.dynamic_slice_in_dim(gain_total, shard_index * gain_width, gain_width, axis=1)
    qkv_grad, out_grad_all, gate_up_grad, down_grad = [
        jnp.stack([layer_grads[layer_no][which] for layer_no in range(LAYER_COUNT)])
        for which in range(4)
    ]
    layer_square = sum(
        (
            jnp.sum(grad_one * grad_one)
            for grad_one in (qkv_grad, out_grad_all, gate_up_grad, down_grad, gain_grad)
        )
    )
    sums = add_all(
        jnp.stack([own_loss, layer_square / ctx_count + jnp.sum(table_grad * table_grad)]),
        ("ctx", "shard"),
    )
    loss_sum, square_sum = sums[0], sums[1]
    grad_norm = jnp.sqrt(square_sum)
    factor = CLIP_NORM / jnp.maximum(grad_norm, CLIP_NORM)
    table_new = advance(embed_table, table_grad, table_mom, table_avg, factor)
    qkv_new = advance(projection_weight, qkv_grad, projection_momentum, projection_average, factor)
    out_new = advance(w_out, out_grad_all, out_mom, out_avg, factor)
    gate_up_new = advance(w_gate_up, gate_up_grad, gate_up_mom, gate_up_avg, factor)
    down_new = advance(w_down, down_grad, down_mom, down_avg, factor)
    gains_new = advance(norm_gains, gain_grad, gain_mom, gain_avg, factor)
    return (
        loss_sum,
        grad_norm,
        table_new[0],
        qkv_new[0],
        out_new[0],
        gate_up_new[0],
        down_new[0],
        gains_new[0],
        table_new[1],
        qkv_new[1],
        out_new[1],
        gate_up_new[1],
        down_new[1],
        gains_new[1],
        table_new[2],
        qkv_new[2],
        out_new[2],
        gate_up_new[2],
        down_new[2],
        gains_new[2],
    )


def solution(mesh):
    return jax.shard_map(
        shards,
        mesh=mesh,
        in_specs=(
            P("shard", "ctx"),
            P("shard", "ctx"),
            P("shard", "ctx"),
            P(("ctx", "shard"), None),
            P(None, "shard", None),
            P(None, "shard", None),
            P(None, "shard", None),
            P(None, "shard", None),
            P(None, "shard"),
            P(("ctx", "shard"), None),
            P(None, "shard", None),
            P(None, "shard", None),
            P(None, "shard", None),
            P(None, "shard", None),
            P(None, "shard"),
            P(("ctx", "shard"), None),
            P(None, "shard", None),
            P(None, "shard", None),
            P(None, "shard", None),
            P(None, "shard", None),
            P(None, "shard"),
        ),
        out_specs=(
            P(),
            P(),
            P(("ctx", "shard"), None),
            P(None, "shard", None),
            P(None, "shard", None),
            P(None, "shard", None),
            P(None, "shard", None),
            P(None, "shard"),
            P(("ctx", "shard"), None),
            P(None, "shard", None),
            P(None, "shard", None),
            P(None, "shard", None),
            P(None, "shard", None),
            P(None, "shard"),
            P(("ctx", "shard"), None),
            P(None, "shard", None),
            P(None, "shard", None),
            P(None, "shard", None),
            P(None, "shard", None),
            P(None, "shard"),
        ),
        check_vma=False,
    )
```

```python
import jax
import jax.numpy as jnp
from jax import lax
from jax.experimental import pallas as pl
from jax.experimental.pallas import tpu as pltpu
from jax.sharding import PartitionSpec as P

MODEL_WIDTH = 576
QUERY_HEADS = 9
KEY_VALUE_HEADS = 3
HEAD_SIZE = 64
FF = 1536
V = 32000
LAYER_COUNT = 2
GROUPS = QUERY_HEADS // KEY_VALUE_HEADS


SMOOTH = 0.1
Z_WEIGHT = 0.0001
CLIP_NORM = 0.08
LEARN_RATE = 100.0
MOMENTUM = 0.5
AVG_DECAY = 0.5
SCORE_SCALE = 0.125
HIDDEN_SCORE = -1e30
EPSILON = 1e-05
HALF_TYPE = jnp.bfloat16
WIDE_NUMBER_TYPE = jnp.float32


def normed(values, gain_row):
    return (
        values * lax.rsqrt(jnp.mean(values * values, axis=-1, keepdims=True) + EPSILON) * gain_row
    )


def rotary(position_row):
    half_dim = HEAD_SIZE // 2
    inv_freq = 10000.0 ** (-jnp.arange(half_dim, dtype=jnp.float32) / half_dim)
    angles = position_row.astype(jnp.float32)[:, None, None] * inv_freq
    return (jnp.cos(angles), jnp.sin(angles))


def rotary_apply(values, cosine_table, sine_values):
    half_dim = HEAD_SIZE // 2
    first_half = values[..., :half_dim]
    second = values[..., half_dim:]
    return jnp.concatenate(
        [
            first_half * cosine_table - second * sine_values,
            second * cosine_table + first_half * sine_values,
        ],
        axis=-1,
    )


def rotate_back(grads_in, cosine_table, sine_values):
    half_dim = HEAD_SIZE // 2
    first_half = grads_in[..., :half_dim]
    second = grads_in[..., half_dim:]
    return jnp.concatenate(
        [
            first_half * cosine_table + second * sine_values,
            second * cosine_table - first_half * sine_values,
        ],
        axis=-1,
    )


def swiglu(gate_up):
    return jax.nn.silu(gate_up[:, :FF]) * gate_up[:, FF:]


def contract(left_side, right_side, left_dim, right_dim):
    return lax.dot_general(
        left_side,
        right_side,
        (((left_dim,), (right_dim,)), ((), ())),
        preferred_element_type=WIDE_NUMBER_TYPE,
    )


def butterfly(values, axis, combine):
    count = lax.axis_size(axis)
    step = 1
    while step < count:
        other = lax.ppermute(values, axis, [(i, i ^ step) for i in range(count)])
        values = combine(values, other)
        step *= 2
    return values


def add_all(values, axes):
    for axis in axes:
        values = butterfly(values, axis, jnp.add)
    return values


def exchange_halves(half_of, axis):
    count = lax.axis_size(axis)
    index = lax.axis_index(axis)
    core = index % 2
    place = index // 2
    leaving = half_of(1 - core)
    half = half_of(core) + lax.ppermute(leaving, axis, [(i, i ^ 1) for i in range(count)])
    half = half.reshape(count // 2, half.shape[0] // (count // 2), half.shape[1])
    total = lax.dynamic_index_in_dim(half, place, axis=0, keepdims=False)
    for step in range(1, count // 2):
        leaving = lax.dynamic_index_in_dim(half, place ^ step, axis=0, keepdims=False)
        sent = lax.ppermute(
            leaving.astype(HALF_TYPE), axis, [(i, i ^ (2 * step)) for i in range(count)]
        )
        total = total + sent.astype(WIDE_NUMBER_TYPE)
    return total


def exchange_sum(partial, axis):
    count = lax.axis_size(axis)
    blocks = partial.reshape(count // 2, 2, partial.shape[0] // count, partial.shape[1])

    def half_of(core):
        half = lax.dynamic_index_in_dim(blocks, core, axis=1, keepdims=False)
        return half.reshape(partial.shape[0] // 2, partial.shape[1])

    return exchange_halves(half_of, axis)


def exchange_product(left_side, right_side, axis):
    count = lax.axis_size(axis)
    width = left_side.shape[1]
    part = width // count
    halves = [
        jnp.concatenate(
            [left_side[:, k * part : (k + 1) * part] for k in range(core, count, 2)], axis=1
        )
        for core in range(2)
    ]

    def half_of(core):
        return contract(jnp.where(core == 0, halves[0], halves[1]), right_side, 0, 0)

    return exchange_halves(half_of, axis)


def window_visible(position_column, key_rows):
    rows = position_column.shape[0]
    base = key_rows - rows
    query_at = lax.broadcasted_iota(jnp.int32, (rows, key_rows), 0) + base
    key_at = lax.broadcasted_iota(jnp.int32, (rows, key_rows), 1)
    return (key_at <= query_at) & (key_at >= query_at - position_column)


def head_slice(head):
    return slice(head * HEAD_SIZE, (head + 1) * HEAD_SIZE)


def attend_kernel(query_ref, key_ref, value_ref, position_ref, out_ref, total_ref):
    key_rows = key_ref.shape[0]
    visible = window_visible(position_ref[...], key_rows)
    for head in range(QUERY_HEADS):
        group = head // GROUPS
        scores = (
            contract(query_ref[:, head_slice(head)], key_ref[:, head_slice(group)], 1, 1)
            * SCORE_SCALE
        )
        scores = jnp.where(visible, scores, HIDDEN_SCORE)
        row_max = jnp.max(scores, axis=1, keepdims=True)
        terms = jnp.exp(scores - row_max)
        row_sum = jnp.sum(terms, axis=1, keepdims=True)
        prob = (terms * (1.0 / row_sum)).astype(HALF_TYPE)
        out_ref[:, head_slice(head)] = contract(
            prob, value_ref[:, head_slice(group)], 1, 0
        ).astype(HALF_TYPE)
        total_ref[:, head : head + 1] = row_max + jnp.log(row_sum)


def attend(query, keys, values, position_column):
    rows = query.shape[0]
    return pl.pallas_call(
        attend_kernel,
        out_shape=(
            jax.ShapeDtypeStruct((rows, QUERY_HEADS * HEAD_SIZE), HALF_TYPE),
            jax.ShapeDtypeStruct((rows, 16), WIDE_NUMBER_TYPE),
        ),
        compiler_params=pltpu.CompilerParams(vmem_limit_bytes=48 << 20),
        name="attend",
    )(query, keys, values, position_column)


def attend_back_kernel(
    query_ref, key_ref, value_ref, total_ref, grad_ref, position_ref, dq_ref, dkv_ref
):
    key_rows = key_ref.shape[0]
    width = KEY_VALUE_HEADS * HEAD_SIZE
    visible = window_visible(position_ref[...], key_rows)
    for group in range(KEY_VALUE_HEADS):
        keys = key_ref[:, head_slice(group)]
        values = value_ref[:, head_slice(group)]
        key_grad = None
        value_grad = None
        for head in range(group * GROUPS, (group + 1) * GROUPS):
            query = query_ref[:, head_slice(head)]
            grad = grad_ref[:, head_slice(head)]
            scores = contract(query, keys, 1, 1) * SCORE_SCALE
            prob = jnp.where(visible, jnp.exp(scores - total_ref[:, head : head + 1]), 0.0)
            grad_prob = contract(grad, values, 1, 1)
            delta = jnp.sum(prob * grad_prob, axis=1, keepdims=True)
            grad_score = (prob * (grad_prob - delta)).astype(HALF_TYPE)
            dq_ref[:, head_slice(head)] = contract(grad_score, keys, 1, 0) * SCORE_SCALE
            key_part = contract(grad_score, query, 0, 0)
            value_part = contract(prob.astype(HALF_TYPE), grad, 0, 0)
            key_grad = key_part if key_grad is None else key_grad + key_part
            value_grad = value_part if value_grad is None else value_grad + value_part
        dkv_ref[:, head_slice(group)] = key_grad * SCORE_SCALE
        dkv_ref[:, width + group * HEAD_SIZE : width + (group + 1) * HEAD_SIZE] = value_grad


def attend_back(query, keys, values, totals, grads, position_column):
    rows = query.shape[0]
    return pl.pallas_call(
        attend_back_kernel,
        out_shape=(
            jax.ShapeDtypeStruct((rows, QUERY_HEADS * HEAD_SIZE), WIDE_NUMBER_TYPE),
            jax.ShapeDtypeStruct(
                (keys.shape[0], 2 * KEY_VALUE_HEADS * HEAD_SIZE), WIDE_NUMBER_TYPE
            ),
        ),
        compiler_params=pltpu.CompilerParams(vmem_limit_bytes=48 << 20),
        name="attend_back",
    )(query, keys, values, totals, grads, position_column)


def stats_kernel(final_ref, target_ref, table_ref, out_ref):
    logits = contract(final_ref[...], table_ref[...], 1, 1)
    row_max = jnp.max(logits, axis=1, keepdims=True)
    exp_sum = jnp.sum(jnp.exp(logits - row_max), axis=1, keepdims=True)
    logit_sum = jnp.sum(logits, axis=1, keepdims=True)
    column = lax.broadcasted_iota(jnp.int32, logits.shape, 1)
    chosen = jnp.sum(jnp.where(column == target_ref[...], logits, 0.0), axis=1, keepdims=True)
    rows = logits.shape[0]
    columns = jnp.concatenate(
        [row_max, exp_sum, logit_sum, chosen, jnp.zeros((rows, 124), WIDE_NUMBER_TYPE)], axis=1
    )
    out_ref[...] = columns.T[:STAT_ROWS]


def combine_kernel(first_ref, second_ref, out_ref):
    joint_max = jnp.maximum(first_ref[0:1], second_ref[0:1])
    out_ref[...] = first_ref[...] + second_ref[...]
    out_ref[0:1] = joint_max
    out_ref[1:2] = first_ref[1:2] * jnp.exp(first_ref[0:1] - joint_max) + second_ref[
        1:2
    ] * jnp.exp(second_ref[0:1] - joint_max)


def combine_stats(first, second):
    return pl.pallas_call(
        combine_kernel,
        out_shape=jax.ShapeDtypeStruct(first.shape, WIDE_NUMBER_TYPE),
        name="combine_stats",
    )(first, second)


STAT_ROWS = 8
TOKEN_TILE = 256


def vocab_stats(finals, target_column, table_rows):
    tokens = finals.shape[0]
    tile = TOKEN_TILE
    return pl.pallas_call(
        stats_kernel,
        grid=(tokens // tile,),
        in_specs=[
            pl.BlockSpec((tile, MODEL_WIDTH), lambda i: (i, 0)),
            pl.BlockSpec((tile, 1), lambda i: (i, 0)),
            pl.BlockSpec(table_rows.shape, lambda i: (0, 0), pipeline_mode=pl.Buffered(1)),
        ],
        out_specs=pl.BlockSpec((STAT_ROWS, tile), lambda i: (0, i)),
        out_shape=jax.ShapeDtypeStruct((STAT_ROWS, tokens), WIDE_NUMBER_TYPE),
        compiler_params=pltpu.CompilerParams(vmem_limit_bytes=56 << 20),
        name="vocab_stats",
    )(finals, target_column, table_rows)


def vocab_grad_kernel(all_tokens, final_ref, target_ref, stat_ref, table_ref, dx_ref, grad_ref):
    finals = final_ref[...]
    table = table_ref[...]
    logits = contract(finals, table, 1, 1)
    lse_row = stat_ref[0:1] + jnp.log(stat_ref[1:2])
    lse = jnp.broadcast_to(lse_row, (128, lse_row.shape[1])).T[:, 0:1]
    column = lax.broadcasted_iota(jnp.int32, logits.shape, 1)
    grad = (
        jnp.exp(logits - lse) * (1.0 + 2.0 * Z_WEIGHT * lse)
        - jnp.where(column == target_ref[...], 1.0 - SMOOTH, 0.0)
        - SMOOTH / V
    ) / all_tokens
    grad = grad.astype(HALF_TYPE)
    grad_ref[...] = grad
    dx_ref[...] = contract(grad, table, 1, 0).astype(HALF_TYPE)


def vocab_grad(finals, target_column, stats, table_rows, all_tokens):
    tokens = finals.shape[0]
    tile = TOKEN_TILE

    def body(*refs):
        vocab_grad_kernel(all_tokens, *refs)

    return pl.pallas_call(
        body,
        grid=(tokens // tile,),
        in_specs=[
            pl.BlockSpec((tile, MODEL_WIDTH), lambda i: (i, 0)),
            pl.BlockSpec((tile, 1), lambda i: (i, 0)),
            pl.BlockSpec((STAT_ROWS, tile), lambda i: (0, i)),
            pl.BlockSpec(table_rows.shape, lambda i: (0, 0), pipeline_mode=pl.Buffered(1)),
        ],
        out_specs=(
            pl.BlockSpec((tile, MODEL_WIDTH), lambda i: (i, 0)),
            pl.BlockSpec((tile, table_rows.shape[0]), lambda i: (i, 0)),
        ),
        out_shape=(
            jax.ShapeDtypeStruct((tokens, MODEL_WIDTH), HALF_TYPE),
            jax.ShapeDtypeStruct((tokens, table_rows.shape[0]), HALF_TYPE),
        ),
        compiler_params=pltpu.CompilerParams(vmem_limit_bytes=60 << 20),
        name="vocab_grad",
    )(finals, target_column, stats, table_rows)


def advance(weight, grad_one, moment, average, factor):
    clipped = grad_one * factor
    moment_new = MOMENTUM * moment + clipped
    weight_new = weight - LEARN_RATE * (clipped + MOMENTUM * moment_new)
    return (weight_new, moment_new, AVG_DECAY * average + (1.0 - AVG_DECAY) * weight_new)


def shards(
    token_ids,
    targets,
    positions,
    embed_table,
    projection_weight,
    w_out,
    w_gate_up,
    w_down,
    norm_gains,
    table_mom,
    projection_momentum,
    out_mom,
    gate_up_mom,
    down_mom,
    gain_mom,
    table_avg,
    projection_average,
    out_avg,
    gate_up_avg,
    down_avg,
    gain_avg,
):
    ctx_count = lax.axis_size("ctx")
    shard_count = lax.axis_size("shard")
    ctx_index = lax.axis_index("ctx")
    shard_index = lax.axis_index("shard")
    token_rows = token_ids.shape[1]
    own_rows = embed_table.shape[0]
    sequence = token_rows * ctx_count
    all_tokens = sequence * shard_count
    query_span_width = QUERY_HEADS * HEAD_SIZE
    key_value_width = KEY_VALUE_HEADS * HEAD_SIZE
    back = ctx_count // 2

    table_rows = lax.all_gather(embed_table.astype(HALF_TYPE), "shard", axis=0, tiled=True)
    slice_rows = table_rows.shape[0]
    pairs = lax.all_gather(
        jnp.concatenate([token_ids, targets], axis=0), ("ctx", "shard"), axis=0
    ).reshape(ctx_count, shard_count, 2, token_rows)
    sequence_pairs = lax.dynamic_index_in_dim(pairs, shard_index, axis=1, keepdims=False)
    first_row = ctx_index * slice_rows
    id_row = sequence_pairs[:, 0].reshape(sequence) - first_row
    target_column = sequence_pairs[:, 1].reshape(sequence, 1) - first_row
    id_here = (id_row >= 0) & (id_row < slice_rows)
    picked = jnp.where(
        id_here[:, None], table_rows[jnp.where(id_here, id_row, 0)], jnp.zeros((), HALF_TYPE)
    )
    looked_up = lax.all_to_all(
        picked.reshape(ctx_count, token_rows, MODEL_WIDTH), "ctx", 0, 0, tiled=True
    )
    hidden = jnp.sum(looked_up.astype(WIDE_NUMBER_TYPE), axis=0)
    position_row = positions[0]
    position_column = position_row[:, None]
    cosine_table, sine_values = rotary(position_row)
    gain_values = lax.all_gather(
        norm_gains.astype(HALF_TYPE), "shard", axis=1, tiled=True
    ).astype(WIDE_NUMBER_TYPE)

    def gathered(weight, layer_id):
        return lax.all_gather(weight[layer_id].astype(HALF_TYPE), "shard", axis=0, tiled=True)

    fetched = [
        tuple(gathered(weight, layer_id) for weight in (projection_weight, w_out, w_gate_up, w_down))
        for layer_id in range(LAYER_COUNT)
    ]

    saved_state = []
    for layer_id in range(LAYER_COUNT):
        qkv_full, out_full, gate_up_full, down_full = fetched[layer_id]
        layer_input = hidden
        attn_in = normed(hidden, gain_values[2 * layer_id]).astype(HALF_TYPE)
        projected_kv = jnp.dot(
            attn_in, qkv_full[:, query_span_width:], preferred_element_type=WIDE_NUMBER_TYPE
        )
        key_rows = (
            rotary_apply(
                projected_kv[:, :key_value_width].reshape(token_rows, KEY_VALUE_HEADS, HEAD_SIZE),
                cosine_table,
                sine_values,
            )
            .astype(HALF_TYPE)
            .reshape(token_rows, key_value_width)
        )
        own_kv = jnp.concatenate(
            [key_rows, projected_kv[:, key_value_width:].astype(HALF_TYPE)], axis=1
        )
        window = [
            lax.ppermute(own_kv, "ctx", [(i, i + step) for i in range(ctx_count - step)])
            for step in range(back, 0, -1)
        ]
        window_kv = jnp.concatenate(window + [own_kv], axis=0)
        window_keys = window_kv[:, :key_value_width]
        window_values = window_kv[:, key_value_width:]
        projected_query = jnp.dot(
            attn_in, qkv_full[:, :query_span_width], preferred_element_type=WIDE_NUMBER_TYPE
        )
        query = (
            rotary_apply(
                projected_query.reshape(token_rows, QUERY_HEADS, HEAD_SIZE),
                cosine_table,
                sine_values,
            )
            .astype(HALF_TYPE)
            .reshape(token_rows, query_span_width)
        )
        attn_out, log_total = attend(query, window_keys, window_values, position_column)
        hidden = hidden + jnp.dot(attn_out, out_full, preferred_element_type=WIDE_NUMBER_TYPE)
        middle = hidden
        mlp_in = normed(hidden, gain_values[2 * layer_id + 1]).astype(HALF_TYPE)
        gate_up = jnp.dot(mlp_in, gate_up_full, preferred_element_type=WIDE_NUMBER_TYPE)
        act_half = swiglu(gate_up).astype(HALF_TYPE)
        hidden = hidden + jnp.dot(act_half, down_full, preferred_element_type=WIDE_NUMBER_TYPE)
        saved_state.append(
            (
                layer_input,
                middle,
                query,
                window_keys,
                window_values,
                log_total,
                attn_out,
                attn_in,
                mlp_in,
                gate_up,
                act_half,
            )
        )
    final_gain = gain_values[2 * LAYER_COUNT]
    final_half = normed(hidden, final_gain).astype(HALF_TYPE)
    sequence_final = lax.all_gather(final_half, "ctx", axis=0, tiled=True)

    stats = vocab_stats(sequence_final, target_column, table_rows)
    stats = butterfly(stats, "ctx", combine_stats)
    hidden_grad_parts, logit_grads = vocab_grad(
        sequence_final, target_column, stats, table_rows, all_tokens
    )
    row_lse = stats[0] + jnp.log(stats[1])
    token_loss = (
        row_lse
        - (1.0 - SMOOTH) * stats[3]
        - SMOOTH * stats[2] / V
        + Z_WEIGHT * row_lse * row_lse
    )
    own_loss = (
        jnp.sum(lax.dynamic_slice_in_dim(token_loss, ctx_index * token_rows, token_rows))
        / all_tokens
    )
    hidden_grad = jnp.sum(
        lax.all_to_all(
            hidden_grad_parts.reshape(ctx_count, token_rows, MODEL_WIDTH), "ctx", 0, 0, tiled=True
        ).astype(WIDE_NUMBER_TYPE),
        axis=0,
    )
    slice_grad = contract(logit_grads, sequence_final, 0, 0)
    _, final_back = jax.vjp(normed, hidden, final_gain)
    grad_hidden, grad_final_gain = final_back(hidden_grad)
    layer_grads = [None] * LAYER_COUNT
    gain_rows = [None] * (2 * LAYER_COUNT) + [grad_final_gain]
    for layer_id in reversed(range(LAYER_COUNT)):
        (
            layer_input,
            middle,
            query,
            window_keys,
            window_values,
            log_total,
            attn_out,
            attn_in,
            mlp_in,
            gate_up,
            act_half,
        ) = saved_state[layer_id]
        qkv_full, out_full, gate_up_full, down_full = fetched[layer_id]
        _, mlp_back = jax.vjp(normed, middle, gain_values[2 * layer_id + 1])
        _, act_back = jax.vjp(swiglu, gate_up)
        out_grad = grad_hidden.astype(HALF_TYPE)
        grad_act = contract(out_grad, down_full, 1, 1)
        grad_gate_up = act_back(grad_act)[0].astype(HALF_TYPE)
        grad_middle, gain_rows[2 * layer_id + 1] = mlp_back(
            contract(grad_gate_up, gate_up_full, 1, 1)
        )
        grad_hidden = grad_hidden + grad_middle
        branch_grad = grad_hidden.astype(HALF_TYPE)
        grad_attended = contract(branch_grad, out_full, 1, 1).astype(HALF_TYPE)
        mlp_grads = (
            exchange_product(mlp_in, grad_gate_up, "shard"),
            exchange_product(act_half, out_grad, "shard"),
        )
        query_gradient, window_grad = attend_back(
            query, window_keys, window_values, log_total, grad_attended, position_column
        )
        key_value_gradient = window_grad[back * token_rows :]
        for step in range(1, back + 1):
            part = window_grad[(back - step) * token_rows : (back - step + 1) * token_rows]
            key_value_gradient = key_value_gradient + lax.ppermute(
                part.astype(HALF_TYPE), "ctx", [(i + step, i) for i in range(ctx_count - step)]
            ).astype(WIDE_NUMBER_TYPE)
        _, attn_back = jax.vjp(normed, layer_input, gain_values[2 * layer_id])
        grad_projected = jnp.concatenate(
            [
                rotate_back(
                    query_gradient.reshape(token_rows, QUERY_HEADS, HEAD_SIZE),
                    cosine_table,
                    sine_values,
                ).reshape(token_rows, query_span_width),
                rotate_back(
                    key_value_gradient[:, :key_value_width].reshape(
                        token_rows, KEY_VALUE_HEADS, HEAD_SIZE
                    ),
                    cosine_table,
                    sine_values,
                ).reshape(token_rows, key_value_width),
                key_value_gradient[:, key_value_width:],
            ],
            axis=1,
        ).astype(HALF_TYPE)
        grad_input, gain_rows[2 * layer_id] = attn_back(contract(grad_projected, qkv_full, 1, 1))
        grad_hidden = grad_hidden + grad_input
        if layer_id > 0:
            mlp_grads, grad_hidden = lax.optimization_barrier((mlp_grads, grad_hidden))
        attn_grads = (
            exchange_product(attn_in, grad_projected, "shard"),
            exchange_product(attn_out, branch_grad, "shard"),
        )
        layer_grads[layer_id] = attn_grads + mlp_grads
    copies = jnp.broadcast_to(
        grad_hidden.astype(HALF_TYPE)[None], (ctx_count, token_rows, MODEL_WIDTH)
    )
    sequence_grad = lax.all_to_all(copies, "ctx", 0, 0, tiled=True).reshape(sequence, MODEL_WIDTH)
    last = LAYER_COUNT - 1
    early = lax.psum(layer_grads[last][2:], "ctx")
    late = tuple(layer_grads[:last]) + (layer_grads[last][:2],)
    early, late, sequence_grad = lax.optimization_barrier((early, late, sequence_grad))
    late = lax.psum(late, "ctx")
    layer_grads = list(late[:last]) + [late[last] + early]
    chosen_rows = jnp.arange(slice_rows)[:, None] == id_row[None, :]
    table_grad = exchange_sum(
        slice_grad + contract(chosen_rows.astype(HALF_TYPE), sequence_grad, 1, 0), "shard"
    )
    gain_total = add_all(jnp.stack(gain_rows), ("ctx", "shard"))
    gain_width = norm_gains.shape[1]
    gain_grad = lax.dynamic_slice_in_dim(gain_total, shard_index * gain_width, gain_width, axis=1)
    qkv_grad, out_grad_all, gate_up_grad, down_grad = [
        jnp.stack([layer_grads[layer_no][which] for layer_no in range(LAYER_COUNT)])
        for which in range(4)
    ]
    layer_square = sum(
        (
            jnp.sum(grad_one * grad_one)
            for grad_one in (qkv_grad, out_grad_all, gate_up_grad, down_grad, gain_grad)
        )
    )
    sums = add_all(
        jnp.stack([own_loss, layer_square / ctx_count + jnp.sum(table_grad * table_grad)]),
        ("ctx", "shard"),
    )
    loss_sum, square_sum = sums[0], sums[1]
    grad_norm = jnp.sqrt(square_sum)
    factor = CLIP_NORM / jnp.maximum(grad_norm, CLIP_NORM)
    table_new = advance(embed_table, table_grad, table_mom, table_avg, factor)
    qkv_new = advance(projection_weight, qkv_grad, projection_momentum, projection_average, factor)
    out_new = advance(w_out, out_grad_all, out_mom, out_avg, factor)
    gate_up_new = advance(w_gate_up, gate_up_grad, gate_up_mom, gate_up_avg, factor)
    down_new = advance(w_down, down_grad, down_mom, down_avg, factor)
    gains_new = advance(norm_gains, gain_grad, gain_mom, gain_avg, factor)
    return (
        loss_sum,
        grad_norm,
        table_new[0],
        qkv_new[0],
        out_new[0],
        gate_up_new[0],
        down_new[0],
        gains_new[0],
        table_new[1],
        qkv_new[1],
        out_new[1],
        gate_up_new[1],
        down_new[1],
        gains_new[1],
        table_new[2],
        qkv_new[2],
        out_new[2],
        gate_up_new[2],
        down_new[2],
        gains_new[2],
    )


def solution(mesh):
    return jax.shard_map(
        shards,
        mesh=mesh,
        in_specs=(
            P("shard", "ctx"),
            P("shard", "ctx"),
            P("shard", "ctx"),
            P(("ctx", "shard"), None),
            P(None, "shard", None),
            P(None, "shard", None),
            P(None, "shard", None),
            P(None, "shard", None),
            P(None, "shard"),
            P(("ctx", "shard"), None),
            P(None, "shard", None),
            P(None, "shard", None),
            P(None, "shard", None),
            P(None, "shard", None),
            P(None, "shard"),
            P(("ctx", "shard"), None),
            P(None, "shard", None),
            P(None, "shard", None),
            P(None, "shard", None),
            P(None, "shard", None),
            P(None, "shard"),
        ),
        out_specs=(
            P(),
            P(),
            P(("ctx", "shard"), None),
            P(None, "shard", None),
            P(None, "shard", None),
            P(None, "shard", None),
            P(None, "shard", None),
            P(None, "shard"),
            P(("ctx", "shard"), None),
            P(None, "shard", None),
            P(None, "shard", None),
            P(None, "shard", None),
            P(None, "shard", None),
            P(None, "shard"),
            P(("ctx", "shard"), None),
            P(None, "shard", None),
            P(None, "shard", None),
            P(None, "shard", None),
            P(None, "shard", None),
            P(None, "shard"),
        ),
        check_vma=False,
    )
```

```python
import jax
import jax.numpy as jnp
from jax import lax
from jax.experimental import pallas as pl
from jax.experimental.pallas import tpu as pltpu
from jax.sharding import PartitionSpec as P

MODEL_WIDTH = 576
QUERY_HEADS = 9
KEY_VALUE_HEADS = 3
HEAD_SIZE = 64
FF = 1536
V = 32000
LAYER_COUNT = 2
GROUPS = QUERY_HEADS // KEY_VALUE_HEADS


SMOOTH = 0.1
Z_WEIGHT = 0.0001
CLIP_NORM = 0.08
LEARN_RATE = 100.0
MOMENTUM = 0.5
AVG_DECAY = 0.5
SCORE_SCALE = 0.125
HIDDEN_SCORE = -1e30
EPSILON = 1e-05
HALF_TYPE = jnp.bfloat16
WIDE_NUMBER_TYPE = jnp.float32


def normed(values, gain_row):
    return (
        values * lax.rsqrt(jnp.mean(values * values, axis=-1, keepdims=True) + EPSILON) * gain_row
    )


def rotary(position_row):
    half_dim = HEAD_SIZE // 2
    inv_freq = 10000.0 ** (-jnp.arange(half_dim, dtype=jnp.float32) / half_dim)
    angles = position_row.astype(jnp.float32)[:, None, None] * inv_freq
    return (jnp.cos(angles), jnp.sin(angles))


def rotary_apply(values, cosine_table, sine_values):
    half_dim = HEAD_SIZE // 2
    first_half = values[..., :half_dim]
    second = values[..., half_dim:]
    return jnp.concatenate(
        [
            first_half * cosine_table - second * sine_values,
            second * cosine_table + first_half * sine_values,
        ],
        axis=-1,
    )


def rotate_back(grads_in, cosine_table, sine_values):
    half_dim = HEAD_SIZE // 2
    first_half = grads_in[..., :half_dim]
    second = grads_in[..., half_dim:]
    return jnp.concatenate(
        [
            first_half * cosine_table + second * sine_values,
            second * cosine_table - first_half * sine_values,
        ],
        axis=-1,
    )


def swiglu(gate_up):
    return jax.nn.silu(gate_up[:, :FF]) * gate_up[:, FF:]


def contract(left_side, right_side, left_dim, right_dim):
    return lax.dot_general(
        left_side,
        right_side,
        (((left_dim,), (right_dim,)), ((), ())),
        preferred_element_type=WIDE_NUMBER_TYPE,
    )


def butterfly(values, axis, combine):
    count = lax.axis_size(axis)
    step = 1
    while step < count:
        other = lax.ppermute(values, axis, [(i, i ^ step) for i in range(count)])
        values = combine(values, other)
        step *= 2
    return values


def add_all(values, axes):
    for axis in axes:
        values = butterfly(values, axis, jnp.add)
    return values


def pair_half(half_of, axis):
    count = lax.axis_size(axis)
    core = lax.axis_index(axis) % 2
    leaving = half_of(1 - core)
    return half_of(core) + lax.ppermute(leaving, axis, [(i, i ^ 1) for i in range(count)])


def own_part(half, axis):
    count = lax.axis_size(axis)
    place = lax.axis_index(axis) // 2
    half = half.reshape(count // 2, half.shape[0] // (count // 2), half.shape[1])
    total = lax.dynamic_index_in_dim(half, place, axis=0, keepdims=False)
    for step in range(1, count // 2):
        leaving = lax.dynamic_index_in_dim(half, place ^ step, axis=0, keepdims=False)
        sent = lax.ppermute(
            leaving.astype(HALF_TYPE), axis, [(i, i ^ (2 * step)) for i in range(count)]
        )
        total = total + sent.astype(WIDE_NUMBER_TYPE)
    return total


def exchange_sum(partial, axis):
    count = lax.axis_size(axis)
    blocks = partial.reshape(count // 2, 2, partial.shape[0] // count, partial.shape[1])

    def half_of(core):
        half = lax.dynamic_index_in_dim(blocks, core, axis=1, keepdims=False)
        return half.reshape(partial.shape[0] // 2, partial.shape[1])

    return own_part(pair_half(half_of, axis), axis)


def product_half(left_side, right_side, axis):
    count = lax.axis_size(axis)
    width = left_side.shape[1]
    part = width // count
    halves = [
        jnp.concatenate(
            [left_side[:, k * part : (k + 1) * part] for k in range(core, count, 2)], axis=1
        )
        for core in range(2)
    ]

    def half_of(core):
        return contract(jnp.where(core == 0, halves[0], halves[1]), right_side, 0, 0)

    return pair_half(half_of, axis)


def window_visible(position_column, key_rows):
    rows = position_column.shape[0]
    base = key_rows - rows
    query_at = lax.broadcasted_iota(jnp.int32, (rows, key_rows), 0) + base
    key_at = lax.broadcasted_iota(jnp.int32, (rows, key_rows), 1)
    return (key_at <= query_at) & (key_at >= query_at - position_column)


def head_slice(head):
    return slice(head * HEAD_SIZE, (head + 1) * HEAD_SIZE)


def attend_kernel(query_ref, key_ref, value_ref, position_ref, out_ref, total_ref):
    key_rows = key_ref.shape[0]
    visible = window_visible(position_ref[...], key_rows)
    for head in range(QUERY_HEADS):
        group = head // GROUPS
        scores = (
            contract(query_ref[:, head_slice(head)], key_ref[:, head_slice(group)], 1, 1)
            * SCORE_SCALE
        )
        scores = jnp.where(visible, scores, HIDDEN_SCORE)
        row_max = jnp.max(scores, axis=1, keepdims=True)
        terms = jnp.exp(scores - row_max)
        row_sum = jnp.sum(terms, axis=1, keepdims=True)
        prob = (terms * (1.0 / row_sum)).astype(HALF_TYPE)
        out_ref[:, head_slice(head)] = contract(
            prob, value_ref[:, head_slice(group)], 1, 0
        ).astype(HALF_TYPE)
        total_ref[:, head : head + 1] = row_max + jnp.log(row_sum)


def attend(query, keys, values, position_column):
    rows = query.shape[0]
    return pl.pallas_call(
        attend_kernel,
        out_shape=(
            jax.ShapeDtypeStruct((rows, QUERY_HEADS * HEAD_SIZE), HALF_TYPE),
            jax.ShapeDtypeStruct((rows, 16), WIDE_NUMBER_TYPE),
        ),
        compiler_params=pltpu.CompilerParams(vmem_limit_bytes=48 << 20),
        name="attend",
    )(query, keys, values, position_column)


def attend_back_kernel(
    query_ref, key_ref, value_ref, total_ref, grad_ref, position_ref, dq_ref, dkv_ref
):
    key_rows = key_ref.shape[0]
    width = KEY_VALUE_HEADS * HEAD_SIZE
    visible = window_visible(position_ref[...], key_rows)
    for group in range(KEY_VALUE_HEADS):
        keys = key_ref[:, head_slice(group)]
        values = value_ref[:, head_slice(group)]
        key_grad = None
        value_grad = None
        for head in range(group * GROUPS, (group + 1) * GROUPS):
            query = query_ref[:, head_slice(head)]
            grad = grad_ref[:, head_slice(head)]
            scores = contract(query, keys, 1, 1) * SCORE_SCALE
            prob = jnp.where(visible, jnp.exp(scores - total_ref[:, head : head + 1]), 0.0)
            grad_prob = contract(grad, values, 1, 1)
            delta = jnp.sum(prob * grad_prob, axis=1, keepdims=True)
            grad_score = (prob * (grad_prob - delta)).astype(HALF_TYPE)
            dq_ref[:, head_slice(head)] = contract(grad_score, keys, 1, 0) * SCORE_SCALE
            key_part = contract(grad_score, query, 0, 0)
            value_part = contract(prob.astype(HALF_TYPE), grad, 0, 0)
            key_grad = key_part if key_grad is None else key_grad + key_part
            value_grad = value_part if value_grad is None else value_grad + value_part
        dkv_ref[:, head_slice(group)] = key_grad * SCORE_SCALE
        dkv_ref[:, width + group * HEAD_SIZE : width + (group + 1) * HEAD_SIZE] = value_grad


def attend_back(query, keys, values, totals, grads, position_column):
    rows = query.shape[0]
    return pl.pallas_call(
        attend_back_kernel,
        out_shape=(
            jax.ShapeDtypeStruct((rows, QUERY_HEADS * HEAD_SIZE), WIDE_NUMBER_TYPE),
            jax.ShapeDtypeStruct(
                (keys.shape[0], 2 * KEY_VALUE_HEADS * HEAD_SIZE), WIDE_NUMBER_TYPE
            ),
        ),
        compiler_params=pltpu.CompilerParams(vmem_limit_bytes=48 << 20),
        name="attend_back",
    )(query, keys, values, totals, grads, position_column)


def stats_kernel(final_ref, target_ref, table_ref, out_ref):
    logits = contract(final_ref[...], table_ref[...], 1, 1)
    row_max = jnp.max(logits, axis=1, keepdims=True)
    exp_sum = jnp.sum(jnp.exp(logits - row_max), axis=1, keepdims=True)
    logit_sum = jnp.sum(logits, axis=1, keepdims=True)
    column = lax.broadcasted_iota(jnp.int32, logits.shape, 1)
    chosen = jnp.sum(jnp.where(column == target_ref[...], logits, 0.0), axis=1, keepdims=True)
    rows = logits.shape[0]
    columns = jnp.concatenate(
        [row_max, exp_sum, logit_sum, chosen, jnp.zeros((rows, 124), WIDE_NUMBER_TYPE)], axis=1
    )
    out_ref[...] = columns.T[:STAT_ROWS]


def combine_kernel(first_ref, second_ref, out_ref):
    joint_max = jnp.maximum(first_ref[0:1], second_ref[0:1])
    out_ref[...] = first_ref[...] + second_ref[...]
    out_ref[0:1] = joint_max
    out_ref[1:2] = first_ref[1:2] * jnp.exp(first_ref[0:1] - joint_max) + second_ref[
        1:2
    ] * jnp.exp(second_ref[0:1] - joint_max)


def combine_stats(first, second):
    return pl.pallas_call(
        combine_kernel,
        out_shape=jax.ShapeDtypeStruct(first.shape, WIDE_NUMBER_TYPE),
        name="combine_stats",
    )(first, second)


STAT_ROWS = 8
TOKEN_TILE = 256


def vocab_stats(finals, target_column, table_rows):
    tokens = finals.shape[0]
    tile = TOKEN_TILE
    return pl.pallas_call(
        stats_kernel,
        grid=(tokens // tile,),
        in_specs=[
            pl.BlockSpec((tile, MODEL_WIDTH), lambda i: (i, 0)),
            pl.BlockSpec((tile, 1), lambda i: (i, 0)),
            pl.BlockSpec(table_rows.shape, lambda i: (0, 0), pipeline_mode=pl.Buffered(1)),
        ],
        out_specs=pl.BlockSpec((STAT_ROWS, tile), lambda i: (0, i)),
        out_shape=jax.ShapeDtypeStruct((STAT_ROWS, tokens), WIDE_NUMBER_TYPE),
        compiler_params=pltpu.CompilerParams(vmem_limit_bytes=56 << 20),
        name="vocab_stats",
    )(finals, target_column, table_rows)


def vocab_grad_kernel(all_tokens, final_ref, target_ref, stat_ref, table_ref, dx_ref, grad_ref):
    finals = final_ref[...]
    table = table_ref[...]
    logits = contract(finals, table, 1, 1)
    lse_row = stat_ref[0:1] + jnp.log(stat_ref[1:2])
    lse = jnp.broadcast_to(lse_row, (128, lse_row.shape[1])).T[:, 0:1]
    column = lax.broadcasted_iota(jnp.int32, logits.shape, 1)
    grad = (
        jnp.exp(logits - lse) * (1.0 + 2.0 * Z_WEIGHT * lse)
        - jnp.where(column == target_ref[...], 1.0 - SMOOTH, 0.0)
        - SMOOTH / V
    ) / all_tokens
    grad = grad.astype(HALF_TYPE)
    grad_ref[...] = grad
    dx_ref[...] = contract(grad, table, 1, 0).astype(HALF_TYPE)


def vocab_grad(finals, target_column, stats, table_rows, all_tokens):
    tokens = finals.shape[0]
    tile = TOKEN_TILE

    def body(*refs):
        vocab_grad_kernel(all_tokens, *refs)

    return pl.pallas_call(
        body,
        grid=(tokens // tile,),
        in_specs=[
            pl.BlockSpec((tile, MODEL_WIDTH), lambda i: (i, 0)),
            pl.BlockSpec((tile, 1), lambda i: (i, 0)),
            pl.BlockSpec((STAT_ROWS, tile), lambda i: (0, i)),
            pl.BlockSpec(table_rows.shape, lambda i: (0, 0), pipeline_mode=pl.Buffered(1)),
        ],
        out_specs=(
            pl.BlockSpec((tile, MODEL_WIDTH), lambda i: (i, 0)),
            pl.BlockSpec((tile, table_rows.shape[0]), lambda i: (i, 0)),
        ),
        out_shape=(
            jax.ShapeDtypeStruct((tokens, MODEL_WIDTH), HALF_TYPE),
            jax.ShapeDtypeStruct((tokens, table_rows.shape[0]), HALF_TYPE),
        ),
        compiler_params=pltpu.CompilerParams(vmem_limit_bytes=60 << 20),
        name="vocab_grad",
    )(finals, target_column, stats, table_rows)


def advance(weight, grad_one, moment, average, factor):
    clipped = grad_one * factor
    moment_new = MOMENTUM * moment + clipped
    weight_new = weight - LEARN_RATE * (clipped + MOMENTUM * moment_new)
    return (weight_new, moment_new, AVG_DECAY * average + (1.0 - AVG_DECAY) * weight_new)


def shards(
    token_ids,
    targets,
    positions,
    embed_table,
    projection_weight,
    w_out,
    w_gate_up,
    w_down,
    norm_gains,
    table_mom,
    projection_momentum,
    out_mom,
    gate_up_mom,
    down_mom,
    gain_mom,
    table_avg,
    projection_average,
    out_avg,
    gate_up_avg,
    down_avg,
    gain_avg,
):
    ctx_count = lax.axis_size("ctx")
    shard_count = lax.axis_size("shard")
    ctx_index = lax.axis_index("ctx")
    shard_index = lax.axis_index("shard")
    token_rows = token_ids.shape[1]
    own_rows = embed_table.shape[0]
    sequence = token_rows * ctx_count
    all_tokens = sequence * shard_count
    query_span_width = QUERY_HEADS * HEAD_SIZE
    key_value_width = KEY_VALUE_HEADS * HEAD_SIZE
    back = ctx_count // 2

    table_rows = lax.all_gather(embed_table.astype(HALF_TYPE), "shard", axis=0, tiled=True)
    slice_rows = table_rows.shape[0]
    pairs = lax.all_gather(
        jnp.concatenate([token_ids, targets], axis=0), ("ctx", "shard"), axis=0
    ).reshape(ctx_count, shard_count, 2, token_rows)
    sequence_pairs = lax.dynamic_index_in_dim(pairs, shard_index, axis=1, keepdims=False)
    first_row = ctx_index * slice_rows
    id_row = sequence_pairs[:, 0].reshape(sequence) - first_row
    target_column = sequence_pairs[:, 1].reshape(sequence, 1) - first_row
    id_here = (id_row >= 0) & (id_row < slice_rows)
    picked = jnp.where(
        id_here[:, None], table_rows[jnp.where(id_here, id_row, 0)], jnp.zeros((), HALF_TYPE)
    )
    looked_up = lax.all_to_all(
        picked.reshape(ctx_count, token_rows, MODEL_WIDTH), "ctx", 0, 0, tiled=True
    )
    hidden = jnp.sum(looked_up.astype(WIDE_NUMBER_TYPE), axis=0)
    position_row = positions[0]
    position_column = position_row[:, None]
    cosine_table, sine_values = rotary(position_row)
    gain_values = lax.all_gather(
        norm_gains.astype(HALF_TYPE), "shard", axis=1, tiled=True
    ).astype(WIDE_NUMBER_TYPE)

    def gathered(weight, layer_id):
        return lax.all_gather(weight[layer_id].astype(HALF_TYPE), "shard", axis=0, tiled=True)

    fetched = [
        tuple(gathered(weight, layer_id) for weight in (projection_weight, w_out, w_gate_up, w_down))
        for layer_id in range(LAYER_COUNT)
    ]

    saved_state = []
    for layer_id in range(LAYER_COUNT):
        qkv_full, out_full, gate_up_full, down_full = fetched[layer_id]
        layer_input = hidden
        attn_in = normed(hidden, gain_values[2 * layer_id]).astype(HALF_TYPE)
        projected_kv = jnp.dot(
            attn_in, qkv_full[:, query_span_width:], preferred_element_type=WIDE_NUMBER_TYPE
        )
        key_rows = (
            rotary_apply(
                projected_kv[:, :key_value_width].reshape(token_rows, KEY_VALUE_HEADS, HEAD_SIZE),
                cosine_table,
                sine_values,
            )
            .astype(HALF_TYPE)
            .reshape(token_rows, key_value_width)
        )
        own_kv = jnp.concatenate(
            [key_rows, projected_kv[:, key_value_width:].astype(HALF_TYPE)], axis=1
        )
        window = [
            lax.ppermute(own_kv, "ctx", [(i, i + step) for i in range(ctx_count - step)])
            for step in range(back, 0, -1)
        ]
        window_kv = jnp.concatenate(window + [own_kv], axis=0)
        window_keys = window_kv[:, :key_value_width]
        window_values = window_kv[:, key_value_width:]
        projected_query = jnp.dot(
            attn_in, qkv_full[:, :query_span_width], preferred_element_type=WIDE_NUMBER_TYPE
        )
        query = (
            rotary_apply(
                projected_query.reshape(token_rows, QUERY_HEADS, HEAD_SIZE),
                cosine_table,
                sine_values,
            )
            .astype(HALF_TYPE)
            .reshape(token_rows, query_span_width)
        )
        attn_out, log_total = attend(query, window_keys, window_values, position_column)
        hidden = hidden + jnp.dot(attn_out, out_full, preferred_element_type=WIDE_NUMBER_TYPE)
        middle = hidden
        mlp_in = normed(hidden, gain_values[2 * layer_id + 1]).astype(HALF_TYPE)
        gate_up = jnp.dot(mlp_in, gate_up_full, preferred_element_type=WIDE_NUMBER_TYPE)
        act_half = swiglu(gate_up).astype(HALF_TYPE)
        hidden = hidden + jnp.dot(act_half, down_full, preferred_element_type=WIDE_NUMBER_TYPE)
        saved_state.append(
            (
                layer_input,
                middle,
                query,
                window_keys,
                window_values,
                log_total,
                attn_out,
                attn_in,
                mlp_in,
                gate_up,
                act_half,
            )
        )
    final_gain = gain_values[2 * LAYER_COUNT]
    final_half = normed(hidden, final_gain).astype(HALF_TYPE)
    sequence_final = lax.all_gather(final_half, "ctx", axis=0, tiled=True)

    stats = vocab_stats(sequence_final, target_column, table_rows)
    stats = butterfly(stats, "ctx", combine_stats)
    hidden_grad_parts, logit_grads = vocab_grad(
        sequence_final, target_column, stats, table_rows, all_tokens
    )
    row_lse = stats[0] + jnp.log(stats[1])
    token_loss = (
        row_lse
        - (1.0 - SMOOTH) * stats[3]
        - SMOOTH * stats[2] / V
        + Z_WEIGHT * row_lse * row_lse
    )
    own_loss = (
        jnp.sum(lax.dynamic_slice_in_dim(token_loss, ctx_index * token_rows, token_rows))
        / all_tokens
    )
    hidden_grad = jnp.sum(
        lax.all_to_all(
            hidden_grad_parts.reshape(ctx_count, token_rows, MODEL_WIDTH), "ctx", 0, 0, tiled=True
        ).astype(WIDE_NUMBER_TYPE),
        axis=0,
    )
    slice_grad = contract(logit_grads, sequence_final, 0, 0)
    hidden_grad, slice_grad = lax.optimization_barrier((hidden_grad, slice_grad))
    _, final_back = jax.vjp(normed, hidden, final_gain)
    grad_hidden, grad_final_gain = final_back(hidden_grad)
    layer_grads = [None] * LAYER_COUNT
    gain_rows = [None] * (2 * LAYER_COUNT) + [grad_final_gain]
    for layer_id in reversed(range(LAYER_COUNT)):
        (
            layer_input,
            middle,
            query,
            window_keys,
            window_values,
            log_total,
            attn_out,
            attn_in,
            mlp_in,
            gate_up,
            act_half,
        ) = saved_state[layer_id]
        qkv_full, out_full, gate_up_full, down_full = fetched[layer_id]
        _, mlp_back = jax.vjp(normed, middle, gain_values[2 * layer_id + 1])
        _, act_back = jax.vjp(swiglu, gate_up)
        out_grad = grad_hidden.astype(HALF_TYPE)
        grad_act = contract(out_grad, down_full, 1, 1)
        grad_gate_up = act_back(grad_act)[0].astype(HALF_TYPE)
        grad_middle, gain_rows[2 * layer_id + 1] = mlp_back(
            contract(grad_gate_up, gate_up_full, 1, 1)
        )
        grad_hidden = grad_hidden + grad_middle
        branch_grad = grad_hidden.astype(HALF_TYPE)
        grad_attended = contract(branch_grad, out_full, 1, 1).astype(HALF_TYPE)
        mlp_halves = (
            product_half(mlp_in, grad_gate_up, "shard"),
            product_half(act_half, out_grad, "shard"),
        )
        query_gradient, window_grad = attend_back(
            query, window_keys, window_values, log_total, grad_attended, position_column
        )
        if layer_id > 0:
            mlp_halves, window_grad = lax.optimization_barrier((mlp_halves, window_grad))
        mlp_grads = tuple(own_part(half, "shard") for half in mlp_halves)
        key_value_gradient = window_grad[back * token_rows :]
        for step in range(1, back + 1):
            part = window_grad[(back - step) * token_rows : (back - step + 1) * token_rows]
            key_value_gradient = key_value_gradient + lax.ppermute(
                part.astype(HALF_TYPE), "ctx", [(i + step, i) for i in range(ctx_count - step)]
            ).astype(WIDE_NUMBER_TYPE)
        _, attn_back = jax.vjp(normed, layer_input, gain_values[2 * layer_id])
        grad_projected = jnp.concatenate(
            [
                rotate_back(
                    query_gradient.reshape(token_rows, QUERY_HEADS, HEAD_SIZE),
                    cosine_table,
                    sine_values,
                ).reshape(token_rows, query_span_width),
                rotate_back(
                    key_value_gradient[:, :key_value_width].reshape(
                        token_rows, KEY_VALUE_HEADS, HEAD_SIZE
                    ),
                    cosine_table,
                    sine_values,
                ).reshape(token_rows, key_value_width),
                key_value_gradient[:, key_value_width:],
            ],
            axis=1,
        ).astype(HALF_TYPE)
        grad_input, gain_rows[2 * layer_id] = attn_back(contract(grad_projected, qkv_full, 1, 1))
        grad_hidden = grad_hidden + grad_input
        if layer_id > 0:
            mlp_grads, grad_hidden = lax.optimization_barrier((mlp_grads, grad_hidden))
        attn_grads = (
            own_part(product_half(attn_in, grad_projected, "shard"), "shard"),
            own_part(product_half(attn_out, branch_grad, "shard"), "shard"),
        )
        layer_grads[layer_id] = attn_grads + mlp_grads
    copies = jnp.broadcast_to(
        grad_hidden.astype(HALF_TYPE)[None], (ctx_count, token_rows, MODEL_WIDTH)
    )
    sequence_grad = lax.all_to_all(copies, "ctx", 0, 0, tiled=True).reshape(sequence, MODEL_WIDTH)
    last = LAYER_COUNT - 1
    early = lax.psum(layer_grads[last][2:], "ctx")
    late = tuple(layer_grads[:last]) + (layer_grads[last][:2],)
    early, late, sequence_grad = lax.optimization_barrier((early, late, sequence_grad))
    late = lax.psum(late, "ctx")
    layer_grads = list(late[:last]) + [late[last] + early]
    chosen_rows = jnp.arange(slice_rows)[:, None] == id_row[None, :]
    table_grad = exchange_sum(
        slice_grad + contract(chosen_rows.astype(HALF_TYPE), sequence_grad, 1, 0), "shard"
    )
    gain_total = add_all(jnp.stack(gain_rows), ("ctx", "shard"))
    gain_width = norm_gains.shape[1]
    gain_grad = lax.dynamic_slice_in_dim(gain_total, shard_index * gain_width, gain_width, axis=1)
    qkv_grad, out_grad_all, gate_up_grad, down_grad = [
        jnp.stack([layer_grads[layer_no][which] for layer_no in range(LAYER_COUNT)])
        for which in range(4)
    ]
    layer_square = sum(
        (
            jnp.sum(grad_one * grad_one)
            for grad_one in (qkv_grad, out_grad_all, gate_up_grad, down_grad, gain_grad)
        )
    )
    sums = add_all(
        jnp.stack([own_loss, layer_square / ctx_count + jnp.sum(table_grad * table_grad)]),
        ("ctx", "shard"),
    )
    loss_sum, square_sum = sums[0], sums[1]
    grad_norm = jnp.sqrt(square_sum)
    factor = CLIP_NORM / jnp.maximum(grad_norm, CLIP_NORM)
    table_new = advance(embed_table, table_grad, table_mom, table_avg, factor)
    qkv_new = advance(projection_weight, qkv_grad, projection_momentum, projection_average, factor)
    out_new = advance(w_out, out_grad_all, out_mom, out_avg, factor)
    gate_up_new = advance(w_gate_up, gate_up_grad, gate_up_mom, gate_up_avg, factor)
    down_new = advance(w_down, down_grad, down_mom, down_avg, factor)
    gains_new = advance(norm_gains, gain_grad, gain_mom, gain_avg, factor)
    return (
        loss_sum,
        grad_norm,
        table_new[0],
        qkv_new[0],
        out_new[0],
        gate_up_new[0],
        down_new[0],
        gains_new[0],
        table_new[1],
        qkv_new[1],
        out_new[1],
        gate_up_new[1],
        down_new[1],
        gains_new[1],
        table_new[2],
        qkv_new[2],
        out_new[2],
        gate_up_new[2],
        down_new[2],
        gains_new[2],
    )


def solution(mesh):
    return jax.shard_map(
        shards,
        mesh=mesh,
        in_specs=(
            P("shard", "ctx"),
            P("shard", "ctx"),
            P("shard", "ctx"),
            P(("ctx", "shard"), None),
            P(None, "shard", None),
            P(None, "shard", None),
            P(None, "shard", None),
            P(None, "shard", None),
            P(None, "shard"),
            P(("ctx", "shard"), None),
            P(None, "shard", None),
            P(None, "shard", None),
            P(None, "shard", None),
            P(None, "shard", None),
            P(None, "shard"),
            P(("ctx", "shard"), None),
            P(None, "shard", None),
            P(None, "shard", None),
            P(None, "shard", None),
            P(None, "shard", None),
            P(None, "shard"),
        ),
        out_specs=(
            P(),
            P(),
            P(("ctx", "shard"), None),
            P(None, "shard", None),
            P(None, "shard", None),
            P(None, "shard", None),
            P(None, "shard", None),
            P(None, "shard"),
            P(("ctx", "shard"), None),
            P(None, "shard", None),
            P(None, "shard", None),
            P(None, "shard", None),
            P(None, "shard", None),
            P(None, "shard"),
            P(("ctx", "shard"), None),
            P(None, "shard", None),
            P(None, "shard", None),
            P(None, "shard", None),
            P(None, "shard", None),
            P(None, "shard"),
        ),
        check_vma=False,
    )
```
